256 devices in a mesh: chart: 32 (over z, y), frame: 8 (over x, core).
Axes of the slice: x: 4, y: 4, z: 8, core: 2. Of those that a mesh axis runs over, the one named last changes fastest.
Arguments:
- features: bfloat16 [16, 512, 64, 128], P('frame', 'chart'), may hold values from -6 to 6
- spatial_a: bfloat16 [3, 3, 64, 64], replicated, may hold values from -0.25 to 0.25
- first_time_kernel: bfloat16 [3, 64, 64], replicated, may hold values from -0.4375 to 0.4375
- spatial_b: bfloat16 [3, 3, 64, 64], replicated, may hold values from -0.25 to 0.25
- second_time_kernel: bfloat16 [3, 64, 64], replicated, may hold values from -0.4375 to 0.4375
- seam_owner: int32 [32, 16], replicated, may hold values from -1 to 31, as said below
- seam_row: int32 [32, 16], replicated, may hold values from -1 to 15
- seam_to: int32 [32, 16], replicated, may hold values from -1 to 15
- grad_out: bfloat16 [16, 512, 64, 128], P('frame', 'chart'), may hold values from -6 to 6
Outputs:
- blended: bfloat16 [16, 512, 64, 128], P('frame', 'chart')
- grad_features: bfloat16 [16, 512, 64, 128], P('frame', 'chart')
- grad_spatial_a: float32 [3, 3, 64, 64], replicated
- grad_temporal_a: float32 [3, 64, 64], replicated
- grad_spatial_b: float32 [3, 3, 64, 64], replicated
- grad_temporal_b: float32 [3, 64, 64], replicated
The draws below stay inside these ranges and needn't reach their ends.
Inputs may be any that keep to these rules, and one draw needn't show every extreme that they name: An entry is empty exactly where seam_owner is -1, and then seam_row and seam_to are -1 as well. A live entry's owner differs from its tile by 1 to 2. At most 4 live entries of one tile share an owner, and every tile has exactly 4 live entries from one owner. Live counts differ from tile to tile.
All inputs are finite; a program needn't handle non-finite values.
Results may differ from the reference program's by a relative error of at most 0.013.
Values may be sent and summed in bfloat16 or wider, within the bound.
A program may use at most 64 MiB of HBM per device.

```python
import jax
import jax.numpy as jnp
from jax import lax

CHANNELS = 64
PIXELS = 128
STRIP_DEV = 16
NEAR_DILATION = 1
REACH = 2
SEAM_CAP = 4
SLOTS = 16
TILES = 32
STRIPS = 512
FRAMES = 16
WIDE_DILATION = 4


def seam_layout(key):
    tile_ids = jnp.arange(TILES, dtype=jnp.int32)[:, None]
    slot_ids = jnp.arange(SLOTS, dtype=jnp.int32)[None, :]
    group_ids = slot_ids // SEAM_CAP
    offsets = jnp.where(group_ids < REACH, group_ids - REACH, group_ids - REACH + 1)
    owners = tile_ids + offsets
    inside_range = (owners >= 0) & (owners < TILES)
    levels = jax.random.randint(jax.random.fold_in(key, 11), (TILES, 1), 0, 5)
    coins = jax.random.randint(jax.random.fold_in(key, 12), (TILES, SLOTS), 0, 4)
    forced = jnp.where(tile_ids < TILES - 1, 1, -1)
    active = inside_range & ((coins < levels) | (offsets == forced))
    sources = jax.random.randint(jax.random.fold_in(key, 13), (TILES, SLOTS), 0, STRIP_DEV)
    targets = jax.random.randint(jax.random.fold_in(key, 14), (TILES, SLOTS), 0, STRIP_DEV)
    owner_list = jnp.where(active, owners, -1).astype(jnp.int32)
    source_list = jnp.where(active, sources, -1).astype(jnp.int32)
    target_list = jnp.where(active, targets, -1).astype(jnp.int32)
    return (owner_list, source_list, target_list)


def draw_seam_owner(key, part):
    return seam_layout(key)[0]


def draw_seam_row(key, part):
    return seam_layout(key)[1]


def draw_seam_to(key, part):
    return seam_layout(key)[2]


def steps_of(own_key, shape, pieces, least, top_value):
    level, own = 1.0, jax.random.fold_in(own_key, 6)
    for position, blocks in pieces:
        draws = jnp.exp(jax.random.uniform(jax.random.fold_in(own, position), (blocks,), jnp.float32, least / len(pieces), top_value / len(pieces)))
        level = level * jnp.repeat(draws, shape[position] // blocks).reshape([-1 if axis == position else 1 for axis in range(len(shape))])
    return level


def normal_values(rng, dims, deviation, reach, pieces=(), kind=jnp.bfloat16):
    values = deviation * jax.random.normal(rng, dims, jnp.float32)
    if pieces:
        values = values * steps_of(rng, dims, pieces, -0.22, 0.18)
    return jnp.clip(values, -reach, reach).astype(kind)


def setup_inputs(seed: int = 0) -> dict:
    keys = jax.random.split(jax.random.key(seed), 10)
    features = normal_values(keys[0], (FRAMES, STRIPS, CHANNELS, PIXELS), 1.0, 6.0, ((0, 8), (1, 32)))
    spatial_a = normal_values(keys[1], (3, 3, CHANNELS, CHANNELS), (9 * CHANNELS) ** -0.5, 0.25)
    first_time_kernel = normal_values(keys[2], (3, CHANNELS, CHANNELS), (3 * CHANNELS) ** -0.5, 0.4375)
    spatial_b = normal_values(keys[3], (3, 3, CHANNELS, CHANNELS), (9 * CHANNELS) ** -0.5, 0.25)
    second_time_kernel = normal_values(keys[4], (3, CHANNELS, CHANNELS), (3 * CHANNELS) ** -0.5, 0.4375)
    seam_owner = draw_seam_owner(jax.random.fold_in(keys[9], 71), 0)
    seam_row = draw_seam_row(jax.random.fold_in(keys[9], 71), 0)
    seam_to = draw_seam_to(jax.random.fold_in(keys[9], 71), 0)
    grad_out = normal_values(keys[8], (FRAMES, STRIPS, CHANNELS, PIXELS), 1.0, 6.0, ((0, 8), (1, 32)))
    return dict(features=features, spatial_a=spatial_a, first_time_kernel=first_time_kernel, spatial_b=spatial_b, second_time_kernel=second_time_kernel, seam_owner=seam_owner, seam_row=seam_row, seam_to=seam_to, grad_out=grad_out)


def silu_slope(values):
    logistic = jax.nn.sigmoid(values)
    return logistic * (1.0 + values * (1.0 - logistic))


def pad_space(values):
    return jnp.pad(values, ((0, 0), (1, 1), (0, 0), (1, 1)))


def temporal_padding(values, spacing):
    return jnp.pad(values, ((spacing, spacing), (0, 0), (0, 0), (0, 0)))


def spatial_apply(padded, weight):
    strips = padded.shape[1] - 2
    pixels = padded.shape[3] - 2
    widened = padded.astype(jnp.float32)
    weights = weight.astype(jnp.float32)
    summed = jnp.zeros((padded.shape[0], strips, weight.shape[2], pixels), jnp.float32)
    for row_tap in range(3):
        for col_tap in range(3):
            summed = summed + jnp.einsum("oc,fscp->fsop", weights[row_tap, col_tap], widened[:, row_tap:row_tap + strips, :, col_tap:col_tap + pixels])
    return summed


def spatial_transpose(padded, weight):
    strips = padded.shape[1] - 2
    pixels = padded.shape[3] - 2
    widened = padded.astype(jnp.float32)
    weights = weight.astype(jnp.float32)
    summed = jnp.zeros((padded.shape[0], strips, weight.shape[3], pixels), jnp.float32)
    for row_tap in range(3):
        for col_tap in range(3):
            summed = summed + jnp.einsum("oc,fsop->fscp", weights[row_tap, col_tap], widened[:, 2 - row_tap:2 - row_tap + strips, :, 2 - col_tap:2 - col_tap + pixels])
    return summed


def spatial_weight(slopes, padded):
    strips = slopes.shape[1]
    pixels = slopes.shape[3]
    slope_wide = slopes.astype(jnp.float32)
    widened = padded.astype(jnp.float32)
    return jnp.stack([jnp.stack([jnp.einsum("fsop,fscp->oc", slope_wide, widened[:, row_tap:row_tap + strips, :, col_tap:col_tap + pixels]) for col_tap in range(3)]) for row_tap in range(3)])


def apply_time_kernel(padded, weight, spacing):
    frames = padded.shape[0] - 2 * spacing
    widened = padded.astype(jnp.float32)
    weights = weight.astype(jnp.float32)
    summed = jnp.zeros((frames, padded.shape[1], weight.shape[1], padded.shape[3]), jnp.float32)
    for kernel_tap in range(3):
        summed = summed + jnp.einsum("oc,fscp->fsop", weights[kernel_tap], widened[kernel_tap * spacing:kernel_tap * spacing + frames])
    return summed


def time_kernel_transposed(padded, weight, spacing):
    frames = padded.shape[0] - 2 * spacing
    widened = padded.astype(jnp.float32)
    weights = weight.astype(jnp.float32)
    summed = jnp.zeros((frames, padded.shape[1], weight.shape[2], padded.shape[3]), jnp.float32)
    for kernel_tap in range(3):
        start_at = (2 - kernel_tap) * spacing
        summed = summed + jnp.einsum("oc,fsop->fscp", weights[kernel_tap], widened[start_at:start_at + frames])
    return summed


def time_kernel_weight(slopes, padded, spacing):
    frames = slopes.shape[0]
    slope_wide = slopes.astype(jnp.float32)
    widened = padded.astype(jnp.float32)
    return jnp.stack([jnp.einsum("fsop,fscp->oc", slope_wide, widened[kernel_tap * spacing:kernel_tap * spacing + frames]) for kernel_tap in range(3)])


def residual_layer(inputs, before):
    return (inputs.astype(jnp.float32) + jax.nn.silu(before)).astype(jnp.bfloat16)


def spatial_layer(inputs, weight):
    def one_frame(single):
        framed = single[None]
        return residual_layer(framed, spatial_apply(pad_space(framed), weight))[0]
    return lax.map(one_frame, inputs)


def spatial_back(upstream, inputs, weight):
    def one_frame(pair):
        grad_frame = pair[0][None]
        input_frame = pair[1][None]
        padded = pad_space(input_frame)
        before = spatial_apply(padded, weight)
        slopes = (grad_frame.astype(jnp.float32) * silu_slope(before)).astype(jnp.bfloat16)
        grad_weight = spatial_weight(slopes, padded)
        result = (grad_frame.astype(jnp.float32) + spatial_transpose(pad_space(slopes), weight)).astype(jnp.bfloat16)
        return result[0], grad_weight
    results, grad_weights = lax.map(one_frame, (upstream, inputs))
    return results, jnp.sum(grad_weights, axis=0)


def temporal_layer(inputs, weight, spacing):
    def one_strip(single):
        stripped = single[:, None]
        before = apply_time_kernel(temporal_padding(stripped, spacing), weight, spacing)
        return residual_layer(stripped, before)[:, 0]
    return jnp.swapaxes(lax.map(one_strip, jnp.swapaxes(inputs, 0, 1)), 0, 1)


def temporal_back(upstream, inputs, weight, spacing):
    def one_strip(pair):
        grad_strip = pair[0][:, None]
        input_strip = pair[1][:, None]
        padded = temporal_padding(input_strip, spacing)
        before = apply_time_kernel(padded, weight, spacing)
        slopes = (grad_strip.astype(jnp.float32) * silu_slope(before)).astype(jnp.bfloat16)
        grad_weight = time_kernel_weight(slopes, padded, spacing)
        result = (grad_strip.astype(jnp.float32) + time_kernel_transposed(temporal_padding(slopes, spacing), weight, spacing)).astype(jnp.bfloat16)
        return result[:, 0], grad_weight
    results, grad_weights = lax.map(one_strip, (jnp.swapaxes(upstream, 0, 1), jnp.swapaxes(inputs, 0, 1)))
    return jnp.swapaxes(results, 0, 1), jnp.sum(grad_weights, axis=0)


def reference(features, spatial_a, first_time_kernel, spatial_b, second_time_kernel, seam_owner, seam_row, seam_to, grad_out):
    first_layer = spatial_layer(features, spatial_a)
    second_layer = temporal_layer(first_layer, first_time_kernel, NEAR_DILATION)
    third_layer = spatial_layer(second_layer, spatial_b)
    layer_four = temporal_layer(third_layer, second_time_kernel, WIDE_DILATION)

    strip_total = features.shape[1]
    active = seam_owner >= 0
    tile_ids = jnp.arange(TILES, dtype=jnp.int32)[:, None]
    sources = jnp.where(active, seam_owner * STRIP_DEV + seam_row, 0).reshape(-1).astype(jnp.int32)
    targets = jnp.where(active, tile_ids * STRIP_DEV + seam_to, 0).reshape(-1).astype(jnp.int32)
    live_weight = active.reshape(-1).astype(jnp.float32)
    strip_ids = jnp.arange(strip_total, dtype=jnp.int32)
    source_hot = (sources[:, None] == strip_ids[None, :]).astype(jnp.float32)
    target_hot = (targets[:, None] == strip_ids[None, :]).astype(jnp.float32) * live_weight[:, None]
    counts = jnp.dot(target_hot.T, source_hot, precision=lax.Precision.HIGHEST)

    def blend_frame(single):
        widened = single.astype(jnp.float32)
        return (widened + jnp.einsum("ts,scp->tcp", counts, widened, precision=lax.Precision.HIGHEST)).astype(jnp.bfloat16)

    def return_frame(single):
        widened = single.astype(jnp.float32)
        return (widened + jnp.einsum("ts,tcp->scp", counts, widened, precision=lax.Precision.HIGHEST)).astype(jnp.bfloat16)

    blended = lax.map(blend_frame, layer_four)
    fourth_gradient = lax.map(return_frame, grad_out)

    third_gradient, gradient_kernel_second = temporal_back(fourth_gradient, third_layer, second_time_kernel, WIDE_DILATION)
    second_gradient, grad_sb = spatial_back(third_gradient, second_layer, spatial_b)
    first_gradient, gradient_kernel_first = temporal_back(second_gradient, first_layer, first_time_kernel, NEAR_DILATION)
    grad_features, grad_sa = spatial_back(first_gradient, features, spatial_a)

    pixel_frames = features.shape[0] * features.shape[1] * features.shape[3]
    grad_scale = float(pixel_frames) ** -0.5
    return blended, grad_features, grad_sa * grad_scale, gradient_kernel_first * grad_scale, grad_sb * grad_scale, gradient_kernel_second * grad_scale
```

```python
import jax
import jax.numpy as jnp
from jax import lax
from jax.sharding import PartitionSpec as P

NEAR_DILATION = 1
REACH = 2
SEAM_CAP = 4


def with_halo(cells, sides, width):
    for axis, dim in sides:
        count = lax.axis_size(axis)
        ends = count - 1
        head = lax.slice_in_dim(cells, 0, width, axis=dim)
        tail = lax.slice_in_dim(cells, cells.shape[dim] - width, cells.shape[dim], axis=dim)
        cells = jnp.concatenate(
            [
                lax.ppermute(tail, axis, [(i, (i + 1) % count) for i in range(ends)]),
                cells,
                lax.ppermute(head, axis, [((i + 1) % count, i) for i in range(ends)]),
            ],
            axis=dim,
        )
    return cells


def from_behind(array, axis, by):
    peers = lax.axis_size(axis)
    pairs = [(i, i + by) for i in range(peers) if 0 <= i + by < peers]
    return lax.ppermute(array, axis, pairs)


def silu_slope(values):
    logistic = jax.nn.sigmoid(values)
    return logistic * (1.0 + values * (1.0 - logistic))


def pad_columns(values):
    return jnp.pad(values, ((0, 0), (0, 0), (0, 0), (1, 1)))


def frames_padding(values, spacing):
    return jnp.pad(values, ((spacing, spacing), (0, 0), (0, 0), (0, 0)))


def chart_rim(values):
    return with_halo(values, (("chart", 1),), 1)


def to_tiles(values):
    return lax.all_to_all(values, "frame", split_axis=1, concat_axis=0, tiled=True)


def to_frames(values):
    return lax.all_to_all(values, "frame", split_axis=0, concat_axis=1, tiled=True)


def near_send(values, steps_by):
    return from_behind(values, "chart", steps_by)


def spatial_apply(padded, weight):
    strips = padded.shape[1] - 2
    pixels = padded.shape[3] - 2
    summed = None
    for row_tap in range(3):
        for col_tap in range(3):
            partial_sum = jnp.einsum(
                "oc,fscp->fsop",
                weight[row_tap, col_tap],
                padded[:, row_tap : row_tap + strips, :, col_tap : col_tap + pixels],
                preferred_element_type=jnp.float32,
            )
            summed = partial_sum if summed is None else summed + partial_sum
    return summed


def spatial_transpose(padded, weight):
    strips = padded.shape[1] - 2
    pixels = padded.shape[3] - 2
    summed = None
    for row_tap in range(3):
        for col_tap in range(3):
            partial_sum = jnp.einsum(
                "oc,fsop->fscp",
                weight[row_tap, col_tap],
                padded[
                    :, 2 - row_tap : 2 - row_tap + strips, :, 2 - col_tap : 2 - col_tap + pixels
                ],
                preferred_element_type=jnp.float32,
            )
            summed = partial_sum if summed is None else summed + partial_sum
    return summed


def spatial_weight(slopes, padded):
    strips = slopes.shape[1]
    pixels = slopes.shape[3]
    return jnp.stack(
        [
            jnp.stack(
                [
                    jnp.einsum(
                        "fsop,fscp->oc",
                        slopes,
                        padded[:, row_tap : row_tap + strips, :, col_tap : col_tap + pixels],
                        preferred_element_type=jnp.float32,
                    )
                    for col_tap in range(3)
                ]
            )
            for row_tap in range(3)
        ]
    )


def apply_time_kernel(padded, weight, spacing):
    frames = padded.shape[0] - 2 * spacing
    summed = None
    for kernel_tap in range(3):
        partial_sum = jnp.einsum(
            "oc,fscp->fsop",
            weight[kernel_tap],
            padded[kernel_tap * spacing : kernel_tap * spacing + frames],
            preferred_element_type=jnp.float32,
        )
        summed = partial_sum if summed is None else summed + partial_sum
    return summed


def time_kernel_transposed(padded, weight, spacing):
    frames = padded.shape[0] - 2 * spacing
    summed = None
    for kernel_tap in range(3):
        start_at = (2 - kernel_tap) * spacing
        partial_sum = jnp.einsum(
            "oc,fsop->fscp",
            weight[kernel_tap],
            padded[start_at : start_at + frames],
            preferred_element_type=jnp.float32,
        )
        summed = partial_sum if summed is None else summed + partial_sum
    return summed


def time_kernel_weight(slopes, padded, spacing):
    frames = slopes.shape[0]
    return jnp.stack(
        [
            jnp.einsum(
                "fsop,fscp->oc",
                slopes,
                padded[kernel_tap * spacing : kernel_tap * spacing + frames],
                preferred_element_type=jnp.float32,
            )
            for kernel_tap in range(3)
        ]
    )


def spatial_forward(inputs, weight, rim_fn):
    padded = pad_columns(rim_fn(inputs))
    before = spatial_apply(padded, weight)
    output = (inputs.astype(jnp.float32) + jax.nn.silu(before)).astype(jnp.bfloat16)
    return (output, before, padded)


def spatial_backward(upstream, before, padded, weight, rim_fn):
    slopes = (upstream.astype(jnp.float32) * silu_slope(before)).astype(jnp.bfloat16)
    grad_weight = spatial_weight(slopes, padded)
    spread = pad_columns(rim_fn(slopes))
    result = (upstream.astype(jnp.float32) + spatial_transpose(spread, weight)).astype(jnp.bfloat16)
    return (result, grad_weight)


def time_kernel_forward(inputs, weight, spacing, time_pad):
    padded = time_pad(inputs, spacing)
    before = apply_time_kernel(padded, weight, spacing)
    output = (inputs.astype(jnp.float32) + jax.nn.silu(before)).astype(jnp.bfloat16)
    return (output, before, padded)


def temporal_backward(upstream, before, padded, weight, spacing, time_pad):
    slopes = (upstream.astype(jnp.float32) * silu_slope(before)).astype(jnp.bfloat16)
    grad_weight = time_kernel_weight(slopes, padded, spacing)
    result = (
        upstream.astype(jnp.float32)
        + time_kernel_transposed(time_pad(slopes, spacing), weight, spacing)
    ).astype(jnp.bfloat16)
    return (result, grad_weight)


def seam_tables(seam_owner, seam_row, seam_to, strips):
    slot_count = seam_owner.shape[1]
    active = seam_owner >= 0
    earlier = jnp.arange(slot_count)[None, :] < jnp.arange(slot_count)[:, None]
    ordinal = jnp.sum((seam_owner[:, :, None] == seam_owner[:, None, :]) & earlier[None], axis=2)
    myself = lax.axis_index("chart")
    rank_hit = (ordinal[:, None, :] == jnp.arange(SEAM_CAP)[None, :, None]) & active[:, None, :]
    as_owner = rank_hit & (seam_owner[:, None, :] == myself)
    send_strip = jnp.sum(jnp.where(as_owner, seam_row[:, None, :], 0), axis=2)
    send_active = jnp.any(as_owner, axis=2)
    own_owner = lax.dynamic_index_in_dim(seam_owner, myself, 0, keepdims=False)
    own_to = lax.dynamic_index_in_dim(seam_to, myself, 0, keepdims=False)
    own_ordinal = lax.dynamic_index_in_dim(ordinal, myself, 0, keepdims=False)
    landing = (own_to[:, None] == jnp.arange(strips)[None, :]).astype(jnp.float32)
    return (send_strip, send_active, own_owner, own_to, own_ordinal, landing)


def receiver_side(tables, owner_ids):
    own_owner, own_to, own_ordinal, landing = (tables[2], tables[3], tables[4], tables[5])
    match_slot = (
        (own_owner[:, None, None] >= 0)
        & (own_owner[:, None, None] == owner_ids[None, :, None])
        & (own_ordinal[:, None, None] == jnp.arange(SEAM_CAP)[None, None, :])
    )
    matrix = jnp.einsum("kt,kqr->tqr", landing, match_slot.astype(jnp.float32))
    back_strip = jnp.sum(jnp.where(match_slot, own_to[:, None, None], 0), axis=0)
    return (matrix, back_strip)


def sender_side(tables, receiver_ids, strips):
    send_strip, send_active = (tables[0], tables[1])
    tile_count = send_strip.shape[0]
    inside_range = (receiver_ids >= 0) & (receiver_ids < tile_count)
    clipped = jnp.clip(receiver_ids, 0, tile_count - 1)
    strip_ids = jnp.take(send_strip, clipped, axis=0)
    live_ids = jnp.take(send_active, clipped, axis=0) & inside_range[:, None]
    matrix = ((strip_ids[None] == jnp.arange(strips)[:, None, None]) & live_ids[None]).astype(
        jnp.float32
    )
    return (strip_ids, matrix)


def pick_strips(values, strip_ids):
    gathered = jnp.take(values, strip_ids.reshape(-1), axis=1)
    return gathered.reshape(
        values.shape[0], strip_ids.shape[0], strip_ids.shape[1], values.shape[2], values.shape[3]
    )


def place_strips(received, matrix):
    return jnp.einsum(
        "tqr,fqrcp->ftcp", matrix.astype(jnp.bfloat16), received, preferred_element_type=jnp.float32
    )


def exchange_sum(parts, axes):
    flat = jnp.concatenate([part.reshape(-1) for part in parts])
    sizes = [lax.axis_size(axis) for axis in axes]
    for axis, size in zip(axes, sizes):
        pieces = flat.reshape(size, -1)
        flat = jnp.sum(lax.all_to_all(pieces, axis, 0, 0, tiled=True), axis=0)
    for axis, size in reversed(list(zip(axes, sizes))):
        copies = jnp.broadcast_to(flat[None], (size,) + flat.shape)
        flat = lax.all_to_all(copies, axis, 0, 0, tiled=True).reshape(-1)
    results = []
    start = 0
    for part in parts:
        results.append(flat[start : start + part.size].reshape(part.shape))
        start += part.size
    return results


def shards(
    features,
    spatial_a,
    first_time_kernel,
    spatial_b,
    second_time_kernel,
    seam_owner,
    seam_row,
    seam_to,
    grad_out,
):
    total_frames = features.shape[0] * lax.axis_size("frame")
    wide_dilation = min(8, total_frames // 4)
    strips = features.shape[1]
    first_layer, pre_one, padded_zero = spatial_forward(features, spatial_a, chart_rim)
    first_layer_tiles = to_tiles(first_layer)
    second_layer, second_preactivation, first_padded = time_kernel_forward(
        first_layer_tiles, first_time_kernel, NEAR_DILATION, frames_padding
    )
    frames_two = to_frames(second_layer)
    frames_three, pre_three, padded_two = spatial_forward(frames_two, spatial_b, chart_rim)
    third_layer = to_tiles(frames_three)
    layer_four, fourth_preactivation, third_padded = time_kernel_forward(
        third_layer, second_time_kernel, wide_dilation, frames_padding
    )
    frames_four = to_frames(layer_four)
    tables = seam_tables(seam_owner, seam_row, seam_to, strips)
    myself = lax.axis_index("chart")
    offsets = [offset for offset in range(-REACH, REACH + 1) if offset != 0]
    offset_array = jnp.array(offsets, dtype=jnp.int32)
    arrivals = []
    for offset in offsets:
        strip_ids, unused_matrix = sender_side(tables, jnp.reshape(myself - offset, (1,)), strips)
        arrivals.append(near_send(pick_strips(frames_four, strip_ids), -offset))
    receive_matrix, back_strip = receiver_side(tables, myself + offset_array)
    moved = place_strips(jnp.concatenate(arrivals, axis=1), receive_matrix)
    returns = []
    for position, offset in enumerate(offsets):
        returns.append(
            near_send(pick_strips(grad_out, back_strip[position : position + 1]), offset)
        )
    unused_ids, return_matrix = sender_side(tables, myself - offset_array, strips)
    moved_back = place_strips(jnp.concatenate(returns, axis=1), return_matrix)
    blended = (frames_four.astype(jnp.float32) + moved).astype(jnp.bfloat16)
    fourth_gradient = (grad_out.astype(jnp.float32) + moved_back).astype(jnp.bfloat16)
    fourth_gradient_tiles = to_tiles(fourth_gradient)
    third_gradient, gradient_kernel_second = temporal_backward(
        fourth_gradient_tiles,
        fourth_preactivation,
        third_padded,
        second_time_kernel,
        wide_dilation,
        frames_padding,
    )
    frames_grad_three = to_frames(third_gradient)
    frames_grad_two, grad_sb = spatial_backward(
        frames_grad_three, pre_three, padded_two, spatial_b, chart_rim
    )
    second_gradient = to_tiles(frames_grad_two)
    first_gradient, gradient_kernel_first = temporal_backward(
        second_gradient,
        second_preactivation,
        first_padded,
        first_time_kernel,
        NEAR_DILATION,
        frames_padding,
    )
    frames_grad_one = to_frames(first_gradient)
    grad_features, grad_sa = spatial_backward(
        frames_grad_one, pre_one, padded_zero, spatial_a, chart_rim
    )
    summed_sa, summed_ta, summed_sb, summed_tb = exchange_sum(
        (grad_sa, gradient_kernel_first, grad_sb, gradient_kernel_second), ("frame", "chart")
    )
    pixel_frames = total_frames * strips * lax.axis_size("chart") * features.shape[3]
    grad_scale = float(pixel_frames) ** (-0.5)
    return (
        blended,
        grad_features,
        summed_sa * grad_scale,
        summed_ta * grad_scale,
        summed_sb * grad_scale,
        summed_tb * grad_scale,
    )


def solution(mesh):
    placed = (
        P("frame", "chart", None, None),
        P(),
        P(),
        P(),
        P(),
        P(),
        P(),
        P(),
        P("frame", "chart", None, None),
    )
    return jax.shard_map(
        shards,
        mesh=mesh,
        in_specs=placed,
        out_specs=(
            P("frame", "chart", None, None),
            P("frame", "chart", None, None),
            P(),
            P(),
            P(),
            P(),
        ),
        check_vma=False,
    )
```

```python
import jax
import jax.numpy as jnp
from jax import lax
from jax.sharding import PartitionSpec as P

NEAR_DILATION = 1
REACH = 2
SEAM_CAP = 4


def with_halo(cells, sides, width):
    for axis, dim in sides:
        count = lax.axis_size(axis)
        ends = count - 1
        head = lax.slice_in_dim(cells, 0, width, axis=dim)
        tail = lax.slice_in_dim(cells, cells.shape[dim] - width, cells.shape[dim], axis=dim)
        cells = jnp.concatenate(
            [
                lax.ppermute(tail, axis, [(i, (i + 1) % count) for i in range(ends)]),
                cells,
                lax.ppermute(head, axis, [((i + 1) % count, i) for i in range(ends)]),
            ],
            axis=dim,
        )
    return cells


def from_behind(array, axis, by):
    peers = lax.axis_size(axis)
    pairs = [(i, i + by) for i in range(peers) if 0 <= i + by < peers]
    return lax.ppermute(array, axis, pairs)


def silu_slope(values):
    logistic = jax.nn.sigmoid(values)
    return logistic * (1.0 + values * (1.0 - logistic))


def pad_columns(values):
    return jnp.pad(values, ((0, 0), (0, 0), (0, 0), (1, 1)))


def chart_rim(values):
    return with_halo(values, (("chart", 1),), 1)


def near_send(values, steps_by):
    return from_behind(values, "chart", steps_by)


def spatial_apply(padded, weight):
    strips = padded.shape[1] - 2
    pixels = padded.shape[3] - 2
    summed = None
    for row_tap in range(3):
        for col_tap in range(3):
            partial_sum = jnp.einsum(
                "oc,fscp->fsop",
                weight[row_tap, col_tap],
                padded[:, row_tap : row_tap + strips, :, col_tap : col_tap + pixels],
                preferred_element_type=jnp.float32,
            )
            summed = partial_sum if summed is None else summed + partial_sum
    return summed


def spatial_transpose(padded, weight):
    strips = padded.shape[1] - 2
    pixels = padded.shape[3] - 2
    summed = None
    for row_tap in range(3):
        for col_tap in range(3):
            partial_sum = jnp.einsum(
                "oc,fsop->fscp",
                weight[row_tap, col_tap],
                padded[
                    :, 2 - row_tap : 2 - row_tap + strips, :, 2 - col_tap : 2 - col_tap + pixels
                ],
                preferred_element_type=jnp.float32,
            )
            summed = partial_sum if summed is None else summed + partial_sum
    return summed


def spatial_weight(slopes, padded):
    strips = slopes.shape[1]
    pixels = slopes.shape[3]
    return jnp.stack(
        [
            jnp.stack(
                [
                    jnp.einsum(
                        "fsop,fscp->oc",
                        slopes,
                        padded[:, row_tap : row_tap + strips, :, col_tap : col_tap + pixels],
                        preferred_element_type=jnp.float32,
                    )
                    for col_tap in range(3)
                ]
            )
            for row_tap in range(3)
        ]
    )


def spatial_forward(inputs, weight, rim_fn):
    padded = pad_columns(rim_fn(inputs))
    before = spatial_apply(padded, weight)
    output = (inputs.astype(jnp.float32) + jax.nn.silu(before)).astype(jnp.bfloat16)
    return (output, before, padded)


def spatial_backward(upstream, before, padded, weight, rim_fn):
    slopes = (upstream.astype(jnp.float32) * silu_slope(before)).astype(jnp.bfloat16)
    grad_weight = spatial_weight(slopes, padded)
    spread = pad_columns(rim_fn(slopes))
    result = (upstream.astype(jnp.float32) + spatial_transpose(spread, weight)).astype(jnp.bfloat16)
    return (result, grad_weight)


def frame_shift(values, offset):
    count = values.shape[0]
    groups = []
    for frame in range(count):
        peer, row = divmod(frame + offset, count)
        if groups and groups[-1][0] == peer:
            groups[-1][2] = row + 1
        else:
            groups.append([peer, row, row + 1])
    pieces = []
    for peer, first, last in groups:
        piece = values[first:last]
        if peer != 0:
            piece = from_behind(piece, "frame", -peer)
        pieces.append(piece)
    return pieces[0] if len(pieces) == 1 else jnp.concatenate(pieces, axis=0)


def time_taps(values, spacing):
    return (frame_shift(values, -spacing), values, frame_shift(values, spacing))


def time_kernel_forward(inputs, weight, spacing):
    taps = time_taps(inputs, spacing)
    before = None
    for kernel_tap in range(3):
        partial_sum = jnp.einsum(
            "oc,fscp->fsop", weight[kernel_tap], taps[kernel_tap], preferred_element_type=jnp.float32
        )
        before = partial_sum if before is None else before + partial_sum
    output = (inputs.astype(jnp.float32) + jax.nn.silu(before)).astype(jnp.bfloat16)
    return (output, before, taps)


def temporal_backward(upstream, before, taps, weight, spacing):
    slopes = (upstream.astype(jnp.float32) * silu_slope(before)).astype(jnp.bfloat16)
    grad_weight = jnp.stack(
        [
            jnp.einsum("fsop,fscp->oc", slopes, taps[kernel_tap], preferred_element_type=jnp.float32)
            for kernel_tap in range(3)
        ]
    )
    spread = time_taps(slopes, spacing)
    summed = upstream.astype(jnp.float32)
    for kernel_tap in range(3):
        summed = summed + jnp.einsum(
            "oc,fsop->fscp",
            weight[kernel_tap],
            spread[2 - kernel_tap],
            preferred_element_type=jnp.float32,
        )
    return (summed.astype(jnp.bfloat16), grad_weight)


def seam_tables(seam_owner, seam_row, seam_to, strips):
    slot_count = seam_owner.shape[1]
    active = seam_owner >= 0
    earlier = jnp.arange(slot_count)[None, :] < jnp.arange(slot_count)[:, None]
    ordinal = jnp.sum((seam_owner[:, :, None] == seam_owner[:, None, :]) & earlier[None], axis=2)
    myself = lax.axis_index("chart")
    rank_hit = (ordinal[:, None, :] == jnp.arange(SEAM_CAP)[None, :, None]) & active[:, None, :]
    as_owner = rank_hit & (seam_owner[:, None, :] == myself)
    send_strip = jnp.sum(jnp.where(as_owner, seam_row[:, None, :], 0), axis=2)
    send_active = jnp.any(as_owner, axis=2)
    own_owner = lax.dynamic_index_in_dim(seam_owner, myself, 0, keepdims=False)
    own_to = lax.dynamic_index_in_dim(seam_to, myself, 0, keepdims=False)
    own_ordinal = lax.dynamic_index_in_dim(ordinal, myself, 0, keepdims=False)
    landing = (own_to[:, None] == jnp.arange(strips)[None, :]).astype(jnp.float32)
    return (send_strip, send_active, own_owner, own_to, own_ordinal, landing)


def receiver_side(tables, owner_ids):
    own_owner, own_to, own_ordinal, landing = (tables[2], tables[3], tables[4], tables[5])
    match_slot = (
        (own_owner[:, None, None] >= 0)
        & (own_owner[:, None, None] == owner_ids[None, :, None])
        & (own_ordinal[:, None, None] == jnp.arange(SEAM_CAP)[None, None, :])
    )
    matrix = jnp.einsum("kt,kqr->tqr", landing, match_slot.astype(jnp.float32))
    back_strip = jnp.sum(jnp.where(match_slot, own_to[:, None, None], 0), axis=0)
    return (matrix, back_strip)


def sender_side(tables, receiver_ids, strips):
    send_strip, send_active = (tables[0], tables[1])
    tile_count = send_strip.shape[0]
    inside_range = (receiver_ids >= 0) & (receiver_ids < tile_count)
    clipped = jnp.clip(receiver_ids, 0, tile_count - 1)
    strip_ids = jnp.take(send_strip, clipped, axis=0)
    live_ids = jnp.take(send_active, clipped, axis=0) & inside_range[:, None]
    matrix = ((strip_ids[None] == jnp.arange(strips)[:, None, None]) & live_ids[None]).astype(
        jnp.float32
    )
    return (strip_ids, matrix)


def pick_strips(values, strip_ids):
    gathered = jnp.take(values, strip_ids.reshape(-1), axis=1)
    return gathered.reshape(
        values.shape[0], strip_ids.shape[0], strip_ids.shape[1], values.shape[2], values.shape[3]
    )


def place_strips(received, matrix):
    return jnp.einsum(
        "tqr,fqrcp->ftcp", matrix.astype(jnp.bfloat16), received, preferred_element_type=jnp.float32
    )


def exchange_sum(parts, axes):
    flat = jnp.concatenate([part.reshape(-1) for part in parts])
    sizes = [lax.axis_size(axis) for axis in axes]
    for axis, size in zip(axes, sizes):
        pieces = flat.reshape(size, -1)
        flat = jnp.sum(lax.all_to_all(pieces, axis, 0, 0, tiled=True), axis=0)
    for axis, size in reversed(list(zip(axes, sizes))):
        copies = jnp.broadcast_to(flat[None], (size,) + flat.shape)
        flat = lax.all_to_all(copies, axis, 0, 0, tiled=True).reshape(-1)
    results = []
    start = 0
    for part in parts:
        results.append(flat[start : start + part.size].reshape(part.shape))
        start += part.size
    return results


def shards(
    features,
    spatial_a,
    first_time_kernel,
    spatial_b,
    second_time_kernel,
    seam_owner,
    seam_row,
    seam_to,
    grad_out,
):
    total_frames = features.shape[0] * lax.axis_size("frame")
    wide_dilation = min(8, total_frames // 4)
    strips = features.shape[1]
    first_layer, pre_one, padded_zero = spatial_forward(features, spatial_a, chart_rim)
    second_layer, second_preactivation, first_padded = time_kernel_forward(
        first_layer, first_time_kernel, NEAR_DILATION
    )
    frames_three, pre_three, padded_two = spatial_forward(second_layer, spatial_b, chart_rim)
    frames_four, fourth_preactivation, third_padded = time_kernel_forward(
        frames_three, second_time_kernel, wide_dilation
    )
    tables = seam_tables(seam_owner, seam_row, seam_to, strips)
    myself = lax.axis_index("chart")
    offsets = [offset for offset in range(-REACH, REACH + 1) if offset != 0]
    offset_array = jnp.array(offsets, dtype=jnp.int32)
    arrivals = []
    for offset in offsets:
        strip_ids, unused_matrix = sender_side(tables, jnp.reshape(myself - offset, (1,)), strips)
        arrivals.append(near_send(pick_strips(frames_four, strip_ids), -offset))
    receive_matrix, back_strip = receiver_side(tables, myself + offset_array)
    moved = place_strips(jnp.concatenate(arrivals, axis=1), receive_matrix)
    returns = []
    for position, offset in enumerate(offsets):
        returns.append(
            near_send(pick_strips(grad_out, back_strip[position : position + 1]), offset)
        )
    unused_ids, return_matrix = sender_side(tables, myself - offset_array, strips)
    moved_back = place_strips(jnp.concatenate(returns, axis=1), return_matrix)
    blended = (frames_four.astype(jnp.float32) + moved).astype(jnp.bfloat16)
    fourth_gradient = (grad_out.astype(jnp.float32) + moved_back).astype(jnp.bfloat16)
    third_gradient, gradient_kernel_second = temporal_backward(
        fourth_gradient,
        fourth_preactivation,
        third_padded,
        second_time_kernel,
        wide_dilation,
    )
    frames_grad_two, grad_sb = spatial_backward(
        third_gradient, pre_three, padded_two, spatial_b, chart_rim
    )
    first_gradient, gradient_kernel_first = temporal_backward(
        frames_grad_two,
        second_preactivation,
        first_padded,
        first_time_kernel,
        NEAR_DILATION,
    )
    grad_features, grad_sa = spatial_backward(
        first_gradient, pre_one, padded_zero, spatial_a, chart_rim
    )
    summed_sa, summed_ta, summed_sb, summed_tb = exchange_sum(
        (grad_sa, gradient_kernel_first, grad_sb, gradient_kernel_second), ("frame", "chart")
    )
    pixel_frames = total_frames * strips * lax.axis_size("chart") * features.shape[3]
    grad_scale = float(pixel_frames) ** (-0.5)
    return (
        blended,
        grad_features,
        summed_sa * grad_scale,
        summed_ta * grad_scale,
        summed_sb * grad_scale,
        summed_tb * grad_scale,
    )


def solution(mesh):
    placed = (
        P("frame", "chart", None, None),
        P(),
        P(),
        P(),
        P(),
        P(),
        P(),
        P(),
        P("frame", "chart", None, None),
    )
    return jax.shard_map(
        shards,
        mesh=mesh,
        in_specs=placed,
        out_specs=(
            P("frame", "chart", None, None),
            P("frame", "chart", None, None),
            P(),
            P(),
            P(),
            P(),
        ),
        check_vma=False,
    )
```

```python
import jax
import jax.numpy as jnp
from jax import lax
from jax.sharding import PartitionSpec as P

NEAR_DILATION = 1
REACH = 2
SEAM_CAP = 4


def with_halo(cells, sides, width):
    for axis, dim in sides:
        count = lax.axis_size(axis)
        ends = count - 1
        head = lax.slice_in_dim(cells, 0, width, axis=dim)
        tail = lax.slice_in_dim(cells, cells.shape[dim] - width, cells.shape[dim], axis=dim)
        cells = jnp.concatenate(
            [
                lax.ppermute(tail, axis, [(i, (i + 1) % count) for i in range(ends)]),
                cells,
                lax.ppermute(head, axis, [((i + 1) % count, i) for i in range(ends)]),
            ],
            axis=dim,
        )
    return cells


def from_behind(array, axis, by):
    peers = lax.axis_size(axis)
    pairs = [(i, i + by) for i in range(peers) if 0 <= i + by < peers]
    return lax.ppermute(array, axis, pairs)


def silu_slope(values):
    logistic = jax.nn.sigmoid(values)
    return logistic * (1.0 + values * (1.0 - logistic))


def pad_columns(values):
    return jnp.pad(values, ((0, 0), (0, 0), (0, 0), (1, 1)))


def chart_rim(values):
    return with_halo(values, (("chart", 1),), 1)


def near_send(values, steps_by):
    return from_behind(values, "chart", steps_by)


def spatial_apply(padded, weight):
    strips = padded.shape[1] - 2
    pixels = padded.shape[3] - 2
    summed = None
    for row_tap in range(3):
        for col_tap in range(3):
            partial_sum = jnp.einsum(
                "oc,fscp->fsop",
                weight[row_tap, col_tap],
                padded[:, row_tap : row_tap + strips, :, col_tap : col_tap + pixels],
                preferred_element_type=jnp.float32,
            )
            summed = partial_sum if summed is None else summed + partial_sum
    return summed


def spatial_transpose(padded, weight):
    strips = padded.shape[1] - 2
    pixels = padded.shape[3] - 2
    summed = None
    for row_tap in range(3):
        for col_tap in range(3):
            partial_sum = jnp.einsum(
                "oc,fsop->fscp",
                weight[row_tap, col_tap],
                padded[
                    :, 2 - row_tap : 2 - row_tap + strips, :, 2 - col_tap : 2 - col_tap + pixels
                ],
                preferred_element_type=jnp.float32,
            )
            summed = partial_sum if summed is None else summed + partial_sum
    return summed


def spatial_weight(slopes, padded):
    strips = slopes.shape[1]
    pixels = slopes.shape[3]
    return jnp.stack(
        [
            jnp.stack(
                [
                    jnp.einsum(
                        "fsop,fscp->oc",
                        slopes,
                        padded[:, row_tap : row_tap + strips, :, col_tap : col_tap + pixels],
                        preferred_element_type=jnp.float32,
                    )
                    for col_tap in range(3)
                ]
            )
            for row_tap in range(3)
        ]
    )


def spatial_forward(inputs, weight, rim_fn):
    padded = pad_columns(rim_fn(inputs))
    before = spatial_apply(padded, weight)
    output = (inputs.astype(jnp.float32) + jax.nn.silu(before)).astype(jnp.bfloat16)
    return (output, before, padded)


def spatial_backward(upstream, before, padded, weight, rim_fn):
    slopes = (upstream.astype(jnp.float32) * silu_slope(before)).astype(jnp.bfloat16)
    grad_weight = spatial_weight(slopes, padded)
    spread = pad_columns(rim_fn(slopes))
    result = (upstream.astype(jnp.float32) + spatial_transpose(spread, weight)).astype(jnp.bfloat16)
    return (result, grad_weight)


def frame_shift(values, offset):
    count = values.shape[0]
    groups = []
    for frame in range(count):
        peer, row = divmod(frame + offset, count)
        if groups and groups[-1][0] == peer:
            groups[-1][2] = row + 1
        else:
            groups.append([peer, row, row + 1])
    pieces = []
    for peer, first, last in groups:
        piece = values[first:last]
        if peer != 0:
            piece = from_behind(piece, "frame", -peer)
        pieces.append(piece)
    return pieces[0] if len(pieces) == 1 else jnp.concatenate(pieces, axis=0)


def time_taps(values, spacing):
    return (frame_shift(values, -spacing), values, frame_shift(values, spacing))


def time_kernel_forward(inputs, weight, spacing):
    taps = time_taps(inputs, spacing)
    before = None
    for kernel_tap in range(3):
        partial_sum = jnp.einsum(
            "oc,fscp->fsop", weight[kernel_tap], taps[kernel_tap], preferred_element_type=jnp.float32
        )
        before = partial_sum if before is None else before + partial_sum
    output = (inputs.astype(jnp.float32) + jax.nn.silu(before)).astype(jnp.bfloat16)
    return (output, before, taps)


def temporal_backward(upstream, before, taps, weight, spacing):
    slopes = (upstream.astype(jnp.float32) * silu_slope(before)).astype(jnp.bfloat16)
    grad_weight = jnp.stack(
        [
            jnp.einsum("fsop,fscp->oc", slopes, taps[kernel_tap], preferred_element_type=jnp.float32)
            for kernel_tap in range(3)
        ]
    )
    spread = time_taps(slopes, spacing)
    summed = upstream.astype(jnp.float32)
    for kernel_tap in range(3):
        summed = summed + jnp.einsum(
            "oc,fsop->fscp",
            weight[kernel_tap],
            spread[2 - kernel_tap],
            preferred_element_type=jnp.float32,
        )
    return (summed.astype(jnp.bfloat16), grad_weight)


def seam_tables(seam_owner, seam_row, seam_to, strips):
    slot_count = seam_owner.shape[1]
    active = seam_owner >= 0
    earlier = jnp.arange(slot_count)[None, :] < jnp.arange(slot_count)[:, None]
    ordinal = jnp.sum((seam_owner[:, :, None] == seam_owner[:, None, :]) & earlier[None], axis=2)
    myself = lax.axis_index("chart")
    rank_hit = (ordinal[:, None, :] == jnp.arange(SEAM_CAP)[None, :, None]) & active[:, None, :]
    as_owner = rank_hit & (seam_owner[:, None, :] == myself)
    send_strip = jnp.sum(jnp.where(as_owner, seam_row[:, None, :], 0), axis=2)
    send_active = jnp.any(as_owner, axis=2)
    own_owner = lax.dynamic_index_in_dim(seam_owner, myself, 0, keepdims=False)
    own_to = lax.dynamic_index_in_dim(seam_to, myself, 0, keepdims=False)
    own_ordinal = lax.dynamic_index_in_dim(ordinal, myself, 0, keepdims=False)
    landing = (own_to[:, None] == jnp.arange(strips)[None, :]).astype(jnp.float32)
    return (send_strip, send_active, own_owner, own_to, own_ordinal, landing)


def receiver_side(tables, owner_ids):
    own_owner, own_to, own_ordinal, landing = (tables[2], tables[3], tables[4], tables[5])
    match_slot = (
        (own_owner[:, None, None] >= 0)
        & (own_owner[:, None, None] == owner_ids[None, :, None])
        & (own_ordinal[:, None, None] == jnp.arange(SEAM_CAP)[None, None, :])
    )
    matrix = jnp.einsum("kt,kqr->tqr", landing, match_slot.astype(jnp.float32))
    back_strip = jnp.sum(jnp.where(match_slot, own_to[:, None, None], 0), axis=0)
    return (matrix, back_strip)


def sender_side(tables, receiver_ids, strips):
    send_strip, send_active = (tables[0], tables[1])
    tile_count = send_strip.shape[0]
    inside_range = (receiver_ids >= 0) & (receiver_ids < tile_count)
    clipped = jnp.clip(receiver_ids, 0, tile_count - 1)
    strip_ids = jnp.take(send_strip, clipped, axis=0)
    live_ids = jnp.take(send_active, clipped, axis=0) & inside_range[:, None]
    matrix = ((strip_ids[None] == jnp.arange(strips)[:, None, None]) & live_ids[None]).astype(
        jnp.float32
    )
    return (strip_ids, matrix)


def pick_strips(values, strip_ids):
    gathered = jnp.take(values, strip_ids.reshape(-1), axis=1)
    return gathered.reshape(
        values.shape[0], strip_ids.shape[0], strip_ids.shape[1], values.shape[2], values.shape[3]
    )


def place_strips(received, matrix):
    return jnp.einsum(
        "tqr,fqrcp->ftcp", matrix.astype(jnp.bfloat16), received, preferred_element_type=jnp.float32
    )


def exchange_sum(parts, axes):
    flat = jnp.concatenate([part.reshape(-1) for part in parts])
    size = 1
    for axis in axes:
        size *= lax.axis_size(axis)
    pieces = flat.reshape(size, -1)
    flat = jnp.sum(lax.all_to_all(pieces, axes, 0, 0, tiled=True), axis=0)
    copies = jnp.broadcast_to(flat[None], (size,) + flat.shape)
    flat = lax.all_to_all(copies, axes, 0, 0, tiled=True).reshape(-1)
    results = []
    start = 0
    for part in parts:
        results.append(flat[start : start + part.size].reshape(part.shape))
        start += part.size
    return results


def shards(
    features,
    spatial_a,
    first_time_kernel,
    spatial_b,
    second_time_kernel,
    seam_owner,
    seam_row,
    seam_to,
    grad_out,
):
    total_frames = features.shape[0] * lax.axis_size("frame")
    wide_dilation = min(8, total_frames // 4)
    strips = features.shape[1]
    first_layer, pre_one, padded_zero = spatial_forward(features, spatial_a, chart_rim)
    second_layer, second_preactivation, first_padded = time_kernel_forward(
        first_layer, first_time_kernel, NEAR_DILATION
    )
    frames_three, pre_three, padded_two = spatial_forward(second_layer, spatial_b, chart_rim)
    frames_four, fourth_preactivation, third_padded = time_kernel_forward(
        frames_three, second_time_kernel, wide_dilation
    )
    tables = seam_tables(seam_owner, seam_row, seam_to, strips)
    myself = lax.axis_index("chart")
    offsets = [offset for offset in range(-REACH, REACH + 1) if offset != 0]
    offset_array = jnp.array(offsets, dtype=jnp.int32)
    arrivals = []
    for offset in offsets:
        strip_ids, unused_matrix = sender_side(tables, jnp.reshape(myself - offset, (1,)), strips)
        arrivals.append(near_send(pick_strips(frames_four, strip_ids), -offset))
    receive_matrix, back_strip = receiver_side(tables, myself + offset_array)
    moved = place_strips(jnp.concatenate(arrivals, axis=1), receive_matrix)
    returns = []
    for position, offset in enumerate(offsets):
        returns.append(
            near_send(pick_strips(grad_out, back_strip[position : position + 1]), offset)
        )
    unused_ids, return_matrix = sender_side(tables, myself - offset_array, strips)
    moved_back = place_strips(jnp.concatenate(returns, axis=1), return_matrix)
    blended = (frames_four.astype(jnp.float32) + moved).astype(jnp.bfloat16)
    fourth_gradient = (grad_out.astype(jnp.float32) + moved_back).astype(jnp.bfloat16)
    third_gradient, gradient_kernel_second = temporal_backward(
        fourth_gradient,
        fourth_preactivation,
        third_padded,
        second_time_kernel,
        wide_dilation,
    )
    frames_grad_two, grad_sb = spatial_backward(
        third_gradient, pre_three, padded_two, spatial_b, chart_rim
    )
    first_gradient, gradient_kernel_first = temporal_backward(
        frames_grad_two,
        second_preactivation,
        first_padded,
        first_time_kernel,
        NEAR_DILATION,
    )
    grad_features, grad_sa = spatial_backward(
        first_gradient, pre_one, padded_zero, spatial_a, chart_rim
    )
    summed_sa, summed_ta, summed_sb, summed_tb = exchange_sum(
        (grad_sa, gradient_kernel_first, grad_sb, gradient_kernel_second), ("frame", "chart")
    )
    pixel_frames = total_frames * strips * lax.axis_size("chart") * features.shape[3]
    grad_scale = float(pixel_frames) ** (-0.5)
    return (
        blended,
        grad_features,
        summed_sa * grad_scale,
        summed_ta * grad_scale,
        summed_sb * grad_scale,
        summed_tb * grad_scale,
    )


def solution(mesh):
    placed = (
        P("frame", "chart", None, None),
        P(),
        P(),
        P(),
        P(),
        P(),
        P(),
        P(),
        P("frame", "chart", None, None),
    )
    return jax.shard_map(
        shards,
        mesh=mesh,
        in_specs=placed,
        out_specs=(
            P("frame", "chart", None, None),
            P("frame", "chart", None, None),
            P(),
            P(),
            P(),
            P(),
        ),
        check_vma=False,
    )
```

```python
import jax
import jax.numpy as jnp
from jax import lax
from jax.sharding import PartitionSpec as P

NEAR_DILATION = 1
REACH = 2
SEAM_CAP = 4


def with_halo(cells, sides, width):
    for axis, dim in sides:
        count = lax.axis_size(axis)
        ends = count - 1
        head = lax.slice_in_dim(cells, 0, width, axis=dim)
        tail = lax.slice_in_dim(cells, cells.shape[dim] - width, cells.shape[dim], axis=dim)
        cells = jnp.concatenate(
            [
                lax.ppermute(tail, axis, [(i, (i + 1) % count) for i in range(ends)]),
                cells,
                lax.ppermute(head, axis, [((i + 1) % count, i) for i in range(ends)]),
            ],
            axis=dim,
        )
    return cells


def from_behind(array, axis, by):
    peers = lax.axis_size(axis)
    pairs = [(i, i + by) for i in range(peers) if 0 <= i + by < peers]
    return lax.ppermute(array, axis, pairs)


def silu_slope(values):
    logistic = jax.nn.sigmoid(values)
    return logistic * (1.0 + values * (1.0 - logistic))


def pad_columns(values):
    return jnp.pad(values, ((0, 0), (0, 0), (0, 0), (1, 1)))


def chart_rim(values):
    return with_halo(values, (("chart", 1),), 1)


def near_send(values, steps_by):
    return from_behind(values, "chart", steps_by)


def spatial_apply(padded, weight):
    strips = padded.shape[1] - 2
    pixels = padded.shape[3] - 2
    summed = None
    for row_tap in range(3):
        for col_tap in range(3):
            partial_sum = jnp.einsum(
                "oc,fscp->fsop",
                weight[row_tap, col_tap],
                padded[:, row_tap : row_tap + strips, :, col_tap : col_tap + pixels],
                preferred_element_type=jnp.float32,
            )
            summed = partial_sum if summed is None else summed + partial_sum
    return summed


def spatial_transpose(padded, weight):
    strips = padded.shape[1] - 2
    pixels = padded.shape[3] - 2
    summed = None
    for row_tap in range(3):
        for col_tap in range(3):
            partial_sum = jnp.einsum(
                "oc,fsop->fscp",
                weight[row_tap, col_tap],
                padded[
                    :, 2 - row_tap : 2 - row_tap + strips, :, 2 - col_tap : 2 - col_tap + pixels
                ],
                preferred_element_type=jnp.float32,
            )
            summed = partial_sum if summed is None else summed + partial_sum
    return summed


def spatial_weight(slopes, padded):
    strips = slopes.shape[1]
    pixels = slopes.shape[3]
    return jnp.stack(
        [
            jnp.stack(
                [
                    jnp.einsum(
                        "fsop,fscp->oc",
                        slopes,
                        padded[:, row_tap : row_tap + strips, :, col_tap : col_tap + pixels],
                        preferred_element_type=jnp.float32,
                    )
                    for col_tap in range(3)
                ]
            )
            for row_tap in range(3)
        ]
    )


def spatial_forward(inputs, weight, rim_fn):
    padded = pad_columns(rim_fn(inputs))
    before = spatial_apply(padded, weight)
    output = (inputs.astype(jnp.float32) + jax.nn.silu(before)).astype(jnp.bfloat16)
    return (output, before, padded)


def spatial_backward(upstream, before, padded, weight, rim_fn):
    slopes = (upstream.astype(jnp.float32) * silu_slope(before)).astype(jnp.bfloat16)
    grad_weight = spatial_weight(slopes, padded)
    spread = pad_columns(rim_fn(slopes))
    result = (upstream.astype(jnp.float32) + spatial_transpose(spread, weight)).astype(jnp.bfloat16)
    return (result, grad_weight)


def frame_shift(values, offset):
    count = values.shape[0]
    groups = []
    for frame in range(count):
        peer, row = divmod(frame + offset, count)
        if groups and groups[-1][0] == peer:
            groups[-1][2] = row + 1
        else:
            groups.append([peer, row, row + 1])
    pieces = []
    for peer, first, last in groups:
        piece = values[first:last]
        if peer != 0:
            piece = from_behind(piece, "frame", -peer)
        pieces.append(piece)
    return pieces[0] if len(pieces) == 1 else jnp.concatenate(pieces, axis=0)


def time_taps(values, spacing):
    return (frame_shift(values, -spacing), values, frame_shift(values, spacing))


def time_kernel_forward(inputs, weight, spacing):
    taps = time_taps(inputs, spacing)
    before = None
    for kernel_tap in range(3):
        partial_sum = jnp.einsum(
            "oc,fscp->fsop", weight[kernel_tap], taps[kernel_tap], preferred_element_type=jnp.float32
        )
        before = partial_sum if before is None else before + partial_sum
    output = (inputs.astype(jnp.float32) + jax.nn.silu(before)).astype(jnp.bfloat16)
    return (output, before, taps)


def temporal_backward(upstream, before, taps, weight, spacing):
    slopes = (upstream.astype(jnp.float32) * silu_slope(before)).astype(jnp.bfloat16)
    grad_weight = jnp.stack(
        [
            jnp.einsum("fsop,fscp->oc", slopes, taps[kernel_tap], preferred_element_type=jnp.float32)
            for kernel_tap in range(3)
        ]
    )
    spread = time_taps(slopes, spacing)
    summed = upstream.astype(jnp.float32)
    for kernel_tap in range(3):
        summed = summed + jnp.einsum(
            "oc,fsop->fscp",
            weight[kernel_tap],
            spread[2 - kernel_tap],
            preferred_element_type=jnp.float32,
        )
    return (summed.astype(jnp.bfloat16), grad_weight)


def seam_tables(seam_owner, seam_row, seam_to, strips):
    slot_count = seam_owner.shape[1]
    active = seam_owner >= 0
    earlier = jnp.arange(slot_count)[None, :] < jnp.arange(slot_count)[:, None]
    ordinal = jnp.sum((seam_owner[:, :, None] == seam_owner[:, None, :]) & earlier[None], axis=2)
    myself = lax.axis_index("chart")
    rank_hit = (ordinal[:, None, :] == jnp.arange(SEAM_CAP)[None, :, None]) & active[:, None, :]
    as_owner = rank_hit & (seam_owner[:, None, :] == myself)
    send_strip = jnp.sum(jnp.where(as_owner, seam_row[:, None, :], 0), axis=2)
    send_active = jnp.any(as_owner, axis=2)
    own_owner = lax.dynamic_index_in_dim(seam_owner, myself, 0, keepdims=False)
    own_to = lax.dynamic_index_in_dim(seam_to, myself, 0, keepdims=False)
    own_ordinal = lax.dynamic_index_in_dim(ordinal, myself, 0, keepdims=False)
    landing = (own_to[:, None] == jnp.arange(strips)[None, :]).astype(jnp.float32)
    return (send_strip, send_active, own_owner, own_to, own_ordinal, landing)


def receiver_side(tables, owner_ids):
    own_owner, own_to, own_ordinal, landing = (tables[2], tables[3], tables[4], tables[5])
    match_slot = (
        (own_owner[:, None, None] >= 0)
        & (own_owner[:, None, None] == owner_ids[None, :, None])
        & (own_ordinal[:, None, None] == jnp.arange(SEAM_CAP)[None, None, :])
    )
    matrix = jnp.einsum("kt,kqr->tqr", landing, match_slot.astype(jnp.float32))
    back_strip = jnp.sum(jnp.where(match_slot, own_to[:, None, None], 0), axis=0)
    return (matrix, back_strip)


def sender_side(tables, receiver_ids, strips):
    send_strip, send_active = (tables[0], tables[1])
    tile_count = send_strip.shape[0]
    inside_range = (receiver_ids >= 0) & (receiver_ids < tile_count)
    clipped = jnp.clip(receiver_ids, 0, tile_count - 1)
    strip_ids = jnp.take(send_strip, clipped, axis=0)
    live_ids = jnp.take(send_active, clipped, axis=0) & inside_range[:, None]
    matrix = ((strip_ids[None] == jnp.arange(strips)[:, None, None]) & live_ids[None]).astype(
        jnp.float32
    )
    return (strip_ids, matrix)


def pick_strips(values, strip_ids):
    gathered = jnp.take(values, strip_ids.reshape(-1), axis=1)
    return gathered.reshape(
        values.shape[0], strip_ids.shape[0], strip_ids.shape[1], values.shape[2], values.shape[3]
    )


def place_strips(received, matrix):
    return jnp.einsum(
        "tqr,fqrcp->ftcp", matrix.astype(jnp.bfloat16), received, preferred_element_type=jnp.float32
    )


def exchange_sum(parts, axes):
    flat = jnp.concatenate([part.reshape(-1) for part in parts])
    size = 1
    for axis in axes:
        size *= lax.axis_size(axis)
    pieces = flat.reshape(size, -1)
    flat = jnp.sum(lax.all_to_all(pieces, axes, 0, 0, tiled=True), axis=0)
    copies = jnp.broadcast_to(flat[None], (size,) + flat.shape)
    flat = lax.all_to_all(copies, axes, 0, 0, tiled=True).reshape(-1)
    results = []
    start = 0
    for part in parts:
        results.append(flat[start : start + part.size].reshape(part.shape))
        start += part.size
    return results


def shards(
    features,
    spatial_a,
    first_time_kernel,
    spatial_b,
    second_time_kernel,
    seam_owner,
    seam_row,
    seam_to,
    grad_out,
):
    total_frames = features.shape[0] * lax.axis_size("frame")
    wide_dilation = min(8, total_frames // 4)
    strips = features.shape[1]
    first_layer, pre_one, padded_zero = spatial_forward(features, spatial_a, chart_rim)
    second_layer, second_preactivation, first_padded = time_kernel_forward(
        first_layer, first_time_kernel, NEAR_DILATION
    )
    frames_three, pre_three, padded_two = spatial_forward(second_layer, spatial_b, chart_rim)
    frames_four, fourth_preactivation, third_padded = time_kernel_forward(
        frames_three, second_time_kernel, wide_dilation
    )
    tables = seam_tables(seam_owner, seam_row, seam_to, strips)
    myself = lax.axis_index("chart")
    offsets = [offset for offset in range(-REACH, REACH + 1) if offset != 0]
    offset_array = jnp.array(offsets, dtype=jnp.int32)
    receive_matrix, back_strip = receiver_side(tables, myself + offset_array)
    outgoing = {}
    for position, offset in enumerate(offsets):
        strip_ids, unused_matrix = sender_side(tables, jnp.reshape(myself - offset, (1,)), strips)
        outgoing[offset] = pick_strips(frames_four, strip_ids)
    arrivals = {}
    returns = {}
    for position, offset in enumerate(offsets):
        going_back = pick_strips(grad_out, back_strip[position : position + 1])
        payload = jnp.concatenate([outgoing[-offset], going_back], axis=1)
        landed = near_send(payload, offset)
        arrivals[-offset] = landed[:, :1]
        returns[offset] = landed[:, 1:]
    moved = place_strips(
        jnp.concatenate([arrivals[offset] for offset in offsets], axis=1), receive_matrix
    )
    unused_ids, return_matrix = sender_side(tables, myself - offset_array, strips)
    moved_back = place_strips(
        jnp.concatenate([returns[offset] for offset in offsets], axis=1), return_matrix
    )
    blended = (frames_four.astype(jnp.float32) + moved).astype(jnp.bfloat16)
    fourth_gradient = (grad_out.astype(jnp.float32) + moved_back).astype(jnp.bfloat16)
    third_gradient, gradient_kernel_second = temporal_backward(
        fourth_gradient,
        fourth_preactivation,
        third_padded,
        second_time_kernel,
        wide_dilation,
    )
    frames_grad_two, grad_sb = spatial_backward(
        third_gradient, pre_three, padded_two, spatial_b, chart_rim
    )
    first_gradient, gradient_kernel_first = temporal_backward(
        frames_grad_two,
        second_preactivation,
        first_padded,
        first_time_kernel,
        NEAR_DILATION,
    )
    grad_features, grad_sa = spatial_backward(
        first_gradient, pre_one, padded_zero, spatial_a, chart_rim
    )
    summed_sa, summed_ta, summed_sb, summed_tb = exchange_sum(
        (grad_sa, gradient_kernel_first, grad_sb, gradient_kernel_second), ("frame", "chart")
    )
    pixel_frames = total_frames * strips * lax.axis_size("chart") * features.shape[3]
    grad_scale = float(pixel_frames) ** (-0.5)
    return (
        blended,
        grad_features,
        summed_sa * grad_scale,
        summed_ta * grad_scale,
        summed_sb * grad_scale,
        summed_tb * grad_scale,
    )


def solution(mesh):
    placed = (
        P("frame", "chart", None, None),
        P(),
        P(),
        P(),
        P(),
        P(),
        P(),
        P(),
        P("frame", "chart", None, None),
    )
    return jax.shard_map(
        shards,
        mesh=mesh,
        in_specs=placed,
        out_specs=(
            P("frame", "chart", None, None),
            P("frame", "chart", None, None),
            P(),
            P(),
            P(),
            P(),
        ),
        check_vma=False,
    )
```

```python
import jax
import jax.numpy as jnp
from jax import lax
from jax.sharding import PartitionSpec as P

NEAR_DILATION = 1
REACH = 2
SEAM_CAP = 4


def with_halo(cells, sides, width):
    for axis, dim in sides:
        count = lax.axis_size(axis)
        ends = count - 1
        head = lax.slice_in_dim(cells, 0, width, axis=dim)
        tail = lax.slice_in_dim(cells, cells.shape[dim] - width, cells.shape[dim], axis=dim)
        cells = jnp.concatenate(
            [
                lax.ppermute(tail, axis, [(i, (i + 1) % count) for i in range(ends)]),
                cells,
                lax.ppermute(head, axis, [((i + 1) % count, i) for i in range(ends)]),
            ],
            axis=dim,
        )
    return cells


def from_behind(array, axis, by):
    peers = lax.axis_size(axis)
    pairs = [(i, i + by) for i in range(peers) if 0 <= i + by < peers]
    return lax.ppermute(array, axis, pairs)


def silu_slope(values):
    logistic = jax.nn.sigmoid(values)
    return logistic * (1.0 + values * (1.0 - logistic))


def pad_columns(values):
    return jnp.pad(values, ((0, 0), (0, 0), (0, 0), (1, 1)))


def chart_rim(values):
    return with_halo(values, (("chart", 1),), 1)


def near_send(values, steps_by):
    return from_behind(values, "chart", steps_by)


def spatial_apply(padded, weight):
    strips = padded.shape[1] - 2
    pixels = padded.shape[3] - 2
    summed = None
    for row_tap in range(3):
        for col_tap in range(3):
            partial_sum = jnp.einsum(
                "oc,fscp->fsop",
                weight[row_tap, col_tap],
                padded[:, row_tap : row_tap + strips, :, col_tap : col_tap + pixels],
                preferred_element_type=jnp.float32,
            )
            summed = partial_sum if summed is None else summed + partial_sum
    return summed


def spatial_transpose(padded, weight):
    strips = padded.shape[1] - 2
    pixels = padded.shape[3] - 2
    summed = None
    for row_tap in range(3):
        for col_tap in range(3):
            partial_sum = jnp.einsum(
                "oc,fsop->fscp",
                weight[row_tap, col_tap],
                padded[
                    :, 2 - row_tap : 2 - row_tap + strips, :, 2 - col_tap : 2 - col_tap + pixels
                ],
                preferred_element_type=jnp.float32,
            )
            summed = partial_sum if summed is None else summed + partial_sum
    return summed


def spatial_weight(slopes, padded):
    strips = slopes.shape[1]
    pixels = slopes.shape[3]
    return jnp.stack(
        [
            jnp.stack(
                [
                    jnp.einsum(
                        "fsop,fscp->oc",
                        slopes,
                        padded[:, row_tap : row_tap + strips, :, col_tap : col_tap + pixels],
                        preferred_element_type=jnp.float32,
                    )
                    for col_tap in range(3)
                ]
            )
            for row_tap in range(3)
        ]
    )


def spatial_forward(inputs, weight, rim_fn):
    padded = pad_columns(rim_fn(inputs))
    before = spatial_apply(padded, weight)
    output = (inputs.astype(jnp.float32) + jax.nn.silu(before)).astype(jnp.bfloat16)
    return (output, before, padded)


def spatial_backward(upstream, before, padded, weight, rim_fn):
    slopes = (upstream.astype(jnp.float32) * silu_slope(before)).astype(jnp.bfloat16)
    grad_weight = spatial_weight(slopes, padded)
    spread = pad_columns(rim_fn(slopes))
    result = (upstream.astype(jnp.float32) + spatial_transpose(spread, weight)).astype(jnp.bfloat16)
    return (result, grad_weight)


def frame_shift(values, offset):
    count = values.shape[0]
    groups = []
    for frame in range(count):
        peer, row = divmod(frame + offset, count)
        if groups and groups[-1][0] == peer:
            groups[-1][2] = row + 1
        else:
            groups.append([peer, row, row + 1])
    pieces = []
    for peer, first, last in groups:
        piece = values[first:last]
        if peer != 0:
            piece = from_behind(piece, "frame", -peer)
        pieces.append(piece)
    return pieces[0] if len(pieces) == 1 else jnp.concatenate(pieces, axis=0)


def time_taps(values, spacing):
    return (frame_shift(values, -spacing), values, frame_shift(values, spacing))


def time_kernel_forward(inputs, weight, spacing):
    taps = time_taps(inputs, spacing)
    before = None
    for kernel_tap in range(3):
        partial_sum = jnp.einsum(
            "oc,fscp->fsop", weight[kernel_tap], taps[kernel_tap], preferred_element_type=jnp.float32
        )
        before = partial_sum if before is None else before + partial_sum
    output = (inputs.astype(jnp.float32) + jax.nn.silu(before)).astype(jnp.bfloat16)
    return (output, before, taps)


def temporal_backward(upstream, before, taps, weight, spacing):
    slopes = (upstream.astype(jnp.float32) * silu_slope(before)).astype(jnp.bfloat16)
    grad_weight = jnp.stack(
        [
            jnp.einsum("fsop,fscp->oc", slopes, taps[kernel_tap], preferred_element_type=jnp.float32)
            for kernel_tap in range(3)
        ]
    )
    spread = time_taps(slopes, spacing)
    summed = upstream.astype(jnp.float32)
    for kernel_tap in range(3):
        summed = summed + jnp.einsum(
            "oc,fsop->fscp",
            weight[kernel_tap],
            spread[2 - kernel_tap],
            preferred_element_type=jnp.float32,
        )
    return (summed.astype(jnp.bfloat16), grad_weight)


def seam_tables(seam_owner, seam_row, seam_to, strips):
    slot_count = seam_owner.shape[1]
    active = seam_owner >= 0
    earlier = jnp.arange(slot_count)[None, :] < jnp.arange(slot_count)[:, None]
    ordinal = jnp.sum((seam_owner[:, :, None] == seam_owner[:, None, :]) & earlier[None], axis=2)
    myself = lax.axis_index("chart")
    rank_hit = (ordinal[:, None, :] == jnp.arange(SEAM_CAP)[None, :, None]) & active[:, None, :]
    as_owner = rank_hit & (seam_owner[:, None, :] == myself)
    send_strip = jnp.sum(jnp.where(as_owner, seam_row[:, None, :], 0), axis=2)
    send_active = jnp.any(as_owner, axis=2)
    own_owner = lax.dynamic_index_in_dim(seam_owner, myself, 0, keepdims=False)
    own_to = lax.dynamic_index_in_dim(seam_to, myself, 0, keepdims=False)
    own_ordinal = lax.dynamic_index_in_dim(ordinal, myself, 0, keepdims=False)
    landing = (own_to[:, None] == jnp.arange(strips)[None, :]).astype(jnp.float32)
    return (send_strip, send_active, own_owner, own_to, own_ordinal, landing)


def receiver_side(tables, owner_ids):
    own_owner, own_to, own_ordinal, landing = (tables[2], tables[3], tables[4], tables[5])
    match_slot = (
        (own_owner[:, None, None] >= 0)
        & (own_owner[:, None, None] == owner_ids[None, :, None])
        & (own_ordinal[:, None, None] == jnp.arange(SEAM_CAP)[None, None, :])
    )
    matrix = jnp.einsum("kt,kqr->tqr", landing, match_slot.astype(jnp.float32))
    back_strip = jnp.sum(jnp.where(match_slot, own_to[:, None, None], 0), axis=0)
    return (matrix, back_strip)


def sender_side(tables, receiver_ids, strips):
    send_strip, send_active = (tables[0], tables[1])
    tile_count = send_strip.shape[0]
    inside_range = (receiver_ids >= 0) & (receiver_ids < tile_count)
    clipped = jnp.clip(receiver_ids, 0, tile_count - 1)
    strip_ids = jnp.take(send_strip, clipped, axis=0)
    live_ids = jnp.take(send_active, clipped, axis=0) & inside_range[:, None]
    matrix = ((strip_ids[None] == jnp.arange(strips)[:, None, None]) & live_ids[None]).astype(
        jnp.float32
    )
    return (strip_ids, matrix)


def pick_strips(values, strip_ids):
    hot = (strip_ids.reshape(-1)[:, None] == jnp.arange(values.shape[1])[None, :]).astype(
        values.dtype
    )
    gathered = jnp.einsum(
        "qs,fscp->fqcp", hot, values, preferred_element_type=jnp.float32
    ).astype(values.dtype)
    return gathered.reshape(
        values.shape[0], strip_ids.shape[0], strip_ids.shape[1], values.shape[2], values.shape[3]
    )


def place_strips(received, matrix):
    return jnp.einsum(
        "tqr,fqrcp->ftcp", matrix.astype(jnp.bfloat16), received, preferred_element_type=jnp.float32
    )


def exchange_sum(parts, axes):
    flat = jnp.concatenate([part.reshape(-1) for part in parts])
    size = 1
    for axis in axes:
        size *= lax.axis_size(axis)
    pieces = flat.reshape(size, -1)
    flat = jnp.sum(lax.all_to_all(pieces, axes, 0, 0, tiled=True), axis=0)
    copies = jnp.broadcast_to(flat[None], (size,) + flat.shape)
    flat = lax.all_to_all(copies, axes, 0, 0, tiled=True).reshape(-1)
    results = []
    start = 0
    for part in parts:
        results.append(flat[start : start + part.size].reshape(part.shape))
        start += part.size
    return results


def shards(
    features,
    spatial_a,
    first_time_kernel,
    spatial_b,
    second_time_kernel,
    seam_owner,
    seam_row,
    seam_to,
    grad_out,
):
    total_frames = features.shape[0] * lax.axis_size("frame")
    wide_dilation = min(8, total_frames // 4)
    strips = features.shape[1]
    first_layer, pre_one, padded_zero = spatial_forward(features, spatial_a, chart_rim)
    second_layer, second_preactivation, first_padded = time_kernel_forward(
        first_layer, first_time_kernel, NEAR_DILATION
    )
    frames_three, pre_three, padded_two = spatial_forward(second_layer, spatial_b, chart_rim)
    frames_four, fourth_preactivation, third_padded = time_kernel_forward(
        frames_three, second_time_kernel, wide_dilation
    )
    tables = seam_tables(seam_owner, seam_row, seam_to, strips)
    myself = lax.axis_index("chart")
    offsets = [offset for offset in range(-REACH, REACH + 1) if offset != 0]
    offset_array = jnp.array(offsets, dtype=jnp.int32)
    receive_matrix, back_strip = receiver_side(tables, myself + offset_array)
    outgoing = {}
    for position, offset in enumerate(offsets):
        strip_ids, unused_matrix = sender_side(tables, jnp.reshape(myself - offset, (1,)), strips)
        outgoing[offset] = pick_strips(frames_four, strip_ids)
    arrivals = {}
    returns = {}
    for position, offset in enumerate(offsets):
        going_back = pick_strips(grad_out, back_strip[position : position + 1])
        payload = jnp.concatenate([outgoing[-offset], going_back], axis=1)
        landed = near_send(payload, offset)
        arrivals[-offset] = landed[:, :1]
        returns[offset] = landed[:, 1:]
    moved = place_strips(
        jnp.concatenate([arrivals[offset] for offset in offsets], axis=1), receive_matrix
    )
    unused_ids, return_matrix = sender_side(tables, myself - offset_array, strips)
    moved_back = place_strips(
        jnp.concatenate([returns[offset] for offset in offsets], axis=1), return_matrix
    )
    blended = (frames_four.astype(jnp.float32) + moved).astype(jnp.bfloat16)
    fourth_gradient = (grad_out.astype(jnp.float32) + moved_back).astype(jnp.bfloat16)
    third_gradient, gradient_kernel_second = temporal_backward(
        fourth_gradient,
        fourth_preactivation,
        third_padded,
        second_time_kernel,
        wide_dilation,
    )
    frames_grad_two, grad_sb = spatial_backward(
        third_gradient, pre_three, padded_two, spatial_b, chart_rim
    )
    first_gradient, gradient_kernel_first = temporal_backward(
        frames_grad_two,
        second_preactivation,
        first_padded,
        first_time_kernel,
        NEAR_DILATION,
    )
    grad_features, grad_sa = spatial_backward(
        first_gradient, pre_one, padded_zero, spatial_a, chart_rim
    )
    summed_sa, summed_ta, summed_sb, summed_tb = exchange_sum(
        (grad_sa, gradient_kernel_first, grad_sb, gradient_kernel_second), ("frame", "chart")
    )
    pixel_frames = total_frames * strips * lax.axis_size("chart") * features.shape[3]
    grad_scale = float(pixel_frames) ** (-0.5)
    return (
        blended,
        grad_features,
        summed_sa * grad_scale,
        summed_ta * grad_scale,
        summed_sb * grad_scale,
        summed_tb * grad_scale,
    )


def solution(mesh):
    placed = (
        P("frame", "chart", None, None),
        P(),
        P(),
        P(),
        P(),
        P(),
        P(),
        P(),
        P("frame", "chart", None, None),
    )
    return jax.shard_map(
        shards,
        mesh=mesh,
        in_specs=placed,
        out_specs=(
            P("frame", "chart", None, None),
            P("frame", "chart", None, None),
            P(),
            P(),
            P(),
            P(),
        ),
        check_vma=False,
    )
```

```python
import jax
import jax.numpy as jnp
from jax import lax
from jax.sharding import PartitionSpec as P

NEAR_DILATION = 1
REACH = 2
SEAM_CAP = 4


def with_halo(cells, sides, width):
    for axis, dim in sides:
        count = lax.axis_size(axis)
        ends = count - 1
        head = lax.slice_in_dim(cells, 0, width, axis=dim)
        tail = lax.slice_in_dim(cells, cells.shape[dim] - width, cells.shape[dim], axis=dim)
        cells = jnp.concatenate(
            [
                lax.ppermute(tail, axis, [(i, (i + 1) % count) for i in range(ends)]),
                cells,
                lax.ppermute(head, axis, [((i + 1) % count, i) for i in range(ends)]),
            ],
            axis=dim,
        )
    return cells


def from_behind(array, axis, by):
    peers = lax.axis_size(axis)
    pairs = [(i, i + by) for i in range(peers) if 0 <= i + by < peers]
    return lax.ppermute(array, axis, pairs)


def silu_slope(values):
    logistic = jax.nn.sigmoid(values)
    return logistic * (1.0 + values * (1.0 - logistic))


def pad_columns(values):
    return jnp.pad(values, ((0, 0), (0, 0), (0, 0), (1, 1)))


def chart_rim(values):
    return with_halo(values, (("chart", 1),), 1)


def near_send(values, steps_by):
    return from_behind(values, "chart", steps_by)


def spatial_apply(padded, weight):
    strips = padded.shape[1] - 2
    pixels = padded.shape[3] - 2
    summed = None
    for row_tap in range(3):
        for col_tap in range(3):
            partial_sum = jnp.einsum(
                "oc,fscp->fsop",
                weight[row_tap, col_tap],
                padded[:, row_tap : row_tap + strips, :, col_tap : col_tap + pixels],
                preferred_element_type=jnp.float32,
            )
            summed = partial_sum if summed is None else summed + partial_sum
    return summed


def spatial_transpose(padded, weight):
    strips = padded.shape[1] - 2
    pixels = padded.shape[3] - 2
    summed = None
    for row_tap in range(3):
        for col_tap in range(3):
            partial_sum = jnp.einsum(
                "oc,fsop->fscp",
                weight[row_tap, col_tap],
                padded[
                    :, 2 - row_tap : 2 - row_tap + strips, :, 2 - col_tap : 2 - col_tap + pixels
                ],
                preferred_element_type=jnp.float32,
            )
            summed = partial_sum if summed is None else summed + partial_sum
    return summed


def spatial_weight(slopes, padded):
    strips = slopes.shape[1]
    pixels = slopes.shape[3]
    return jnp.stack(
        [
            jnp.stack(
                [
                    jnp.einsum(
                        "fsop,fscp->oc",
                        slopes,
                        padded[:, row_tap : row_tap + strips, :, col_tap : col_tap + pixels],
                        preferred_element_type=jnp.float32,
                    )
                    for col_tap in range(3)
                ]
            )
            for row_tap in range(3)
        ]
    )


def spatial_forward(inputs, weight, rim_fn):
    padded = pad_columns(rim_fn(inputs))
    before = spatial_apply(padded, weight)
    output = (inputs.astype(jnp.float32) + jax.nn.silu(before)).astype(jnp.bfloat16)
    return (output, before, padded)


def spatial_backward(upstream, before, padded, weight, rim_fn):
    slopes = (upstream.astype(jnp.float32) * silu_slope(before)).astype(jnp.bfloat16)
    grad_weight = spatial_weight(slopes, padded)
    spread = pad_columns(rim_fn(slopes))
    result = (upstream.astype(jnp.float32) + spatial_transpose(spread, weight)).astype(jnp.bfloat16)
    return (result, grad_weight)


def frame_shift(values, offset):
    count = values.shape[0]
    groups = []
    for frame in range(count):
        peer, row = divmod(frame + offset, count)
        if groups and groups[-1][0] == peer:
            groups[-1][2] = row + 1
        else:
            groups.append([peer, row, row + 1])
    pieces = []
    for peer, first, last in groups:
        piece = values[first:last]
        if peer != 0:
            piece = from_behind(piece, "frame", -peer)
        pieces.append(piece)
    return pieces[0] if len(pieces) == 1 else jnp.concatenate(pieces, axis=0)


def time_taps(values, spacing):
    return (frame_shift(values, -spacing), values, frame_shift(values, spacing))


def time_kernel_forward(inputs, weight, spacing):
    taps = time_taps(inputs, spacing)
    before = None
    for kernel_tap in range(3):
        partial_sum = jnp.einsum(
            "oc,fscp->fsop", weight[kernel_tap], taps[kernel_tap], preferred_element_type=jnp.float32
        )
        before = partial_sum if before is None else before + partial_sum
    output = (inputs.astype(jnp.float32) + jax.nn.silu(before)).astype(jnp.bfloat16)
    return (output, before, taps)


def temporal_backward(upstream, before, taps, weight, spacing):
    slopes = (upstream.astype(jnp.float32) * silu_slope(before)).astype(jnp.bfloat16)
    grad_weight = jnp.stack(
        [
            jnp.einsum("fsop,fscp->oc", slopes, taps[kernel_tap], preferred_element_type=jnp.float32)
            for kernel_tap in range(3)
        ]
    )
    spread = time_taps(slopes, spacing)
    summed = upstream.astype(jnp.float32)
    for kernel_tap in range(3):
        summed = summed + jnp.einsum(
            "oc,fsop->fscp",
            weight[kernel_tap],
            spread[2 - kernel_tap],
            preferred_element_type=jnp.float32,
        )
    return (summed.astype(jnp.bfloat16), grad_weight)


def seam_tables(seam_owner, seam_row, seam_to, strips):
    slot_count = seam_owner.shape[1]
    active = seam_owner >= 0
    earlier = jnp.arange(slot_count)[None, :] < jnp.arange(slot_count)[:, None]
    ordinal = jnp.sum((seam_owner[:, :, None] == seam_owner[:, None, :]) & earlier[None], axis=2)
    myself = lax.axis_index("chart")
    rank_hit = (ordinal[:, None, :] == jnp.arange(SEAM_CAP)[None, :, None]) & active[:, None, :]
    as_owner = rank_hit & (seam_owner[:, None, :] == myself)
    send_strip = jnp.sum(jnp.where(as_owner, seam_row[:, None, :], 0), axis=2)
    send_active = jnp.any(as_owner, axis=2)
    own_owner = lax.dynamic_index_in_dim(seam_owner, myself, 0, keepdims=False)
    own_to = lax.dynamic_index_in_dim(seam_to, myself, 0, keepdims=False)
    own_ordinal = lax.dynamic_index_in_dim(ordinal, myself, 0, keepdims=False)
    landing = (own_to[:, None] == jnp.arange(strips)[None, :]).astype(jnp.float32)
    return (send_strip, send_active, own_owner, own_to, own_ordinal, landing)


def receiver_side(tables, owner_ids):
    own_owner, own_to, own_ordinal, landing = (tables[2], tables[3], tables[4], tables[5])
    match_slot = (
        (own_owner[:, None, None] >= 0)
        & (own_owner[:, None, None] == owner_ids[None, :, None])
        & (own_ordinal[:, None, None] == jnp.arange(SEAM_CAP)[None, None, :])
    )
    matrix = jnp.einsum("kt,kqr->tqr", landing, match_slot.astype(jnp.float32))
    back_strip = jnp.sum(jnp.where(match_slot, own_to[:, None, None], 0), axis=0)
    return (matrix, back_strip)


def sender_side(tables, receiver_ids, strips):
    send_strip, send_active = (tables[0], tables[1])
    tile_count = send_strip.shape[0]
    inside_range = (receiver_ids >= 0) & (receiver_ids < tile_count)
    clipped = jnp.clip(receiver_ids, 0, tile_count - 1)
    strip_ids = jnp.take(send_strip, clipped, axis=0)
    live_ids = jnp.take(send_active, clipped, axis=0) & inside_range[:, None]
    matrix = ((strip_ids[None] == jnp.arange(strips)[:, None, None]) & live_ids[None]).astype(
        jnp.float32
    )
    return (strip_ids, matrix)


def pick_strips(values, strip_ids):
    hot = (strip_ids.reshape(-1)[:, None] == jnp.arange(values.shape[1])[None, :]).astype(
        values.dtype
    )
    gathered = jnp.einsum(
        "qs,fscp->fqcp", hot, values, preferred_element_type=jnp.float32
    ).astype(values.dtype)
    return gathered.reshape(
        values.shape[0], strip_ids.shape[0], strip_ids.shape[1], values.shape[2], values.shape[3]
    )


def place_strips(received, matrix):
    return jnp.einsum(
        "tqr,fqrcp->ftcp", matrix.astype(jnp.bfloat16), received, preferred_element_type=jnp.float32
    )


def exchange_sum(parts, axes, scale):
    flat = jnp.concatenate([part.reshape(-1) for part in parts]) * scale
    size = 1
    for axis in axes:
        size *= lax.axis_size(axis)
    pieces = flat.reshape(size, -1)
    flat = jnp.sum(lax.all_to_all(pieces, axes, 0, 0, tiled=True), axis=0)
    copies = jnp.broadcast_to(flat[None], (size,) + flat.shape)
    flat = lax.all_to_all(copies, axes, 0, 0, tiled=True).reshape(-1)
    results = []
    start = 0
    for part in parts:
        results.append(flat[start : start + part.size].reshape(part.shape))
        start += part.size
    return results


def shards(
    features,
    spatial_a,
    first_time_kernel,
    spatial_b,
    second_time_kernel,
    seam_owner,
    seam_row,
    seam_to,
    grad_out,
):
    total_frames = features.shape[0] * lax.axis_size("frame")
    wide_dilation = min(8, total_frames // 4)
    strips = features.shape[1]
    first_layer, pre_one, padded_zero = spatial_forward(features, spatial_a, chart_rim)
    second_layer, second_preactivation, first_padded = time_kernel_forward(
        first_layer, first_time_kernel, NEAR_DILATION
    )
    frames_three, pre_three, padded_two = spatial_forward(second_layer, spatial_b, chart_rim)
    frames_four, fourth_preactivation, third_padded = time_kernel_forward(
        frames_three, second_time_kernel, wide_dilation
    )
    tables = seam_tables(seam_owner, seam_row, seam_to, strips)
    myself = lax.axis_index("chart")
    offsets = [offset for offset in range(-REACH, REACH + 1) if offset != 0]
    offset_array = jnp.array(offsets, dtype=jnp.int32)
    receive_matrix, back_strip = receiver_side(tables, myself + offset_array)
    outgoing = {}
    for position, offset in enumerate(offsets):
        strip_ids, unused_matrix = sender_side(tables, jnp.reshape(myself - offset, (1,)), strips)
        outgoing[offset] = pick_strips(frames_four, strip_ids)
    arrivals = {}
    returns = {}
    for position, offset in enumerate(offsets):
        going_back = pick_strips(grad_out, back_strip[position : position + 1])
        payload = jnp.concatenate([outgoing[-offset], going_back], axis=1)
        landed = near_send(payload, offset)
        arrivals[-offset] = landed[:, :1]
        returns[offset] = landed[:, 1:]
    moved = place_strips(
        jnp.concatenate([arrivals[offset] for offset in offsets], axis=1), receive_matrix
    )
    unused_ids, return_matrix = sender_side(tables, myself - offset_array, strips)
    moved_back = place_strips(
        jnp.concatenate([returns[offset] for offset in offsets], axis=1), return_matrix
    )
    blended = (frames_four.astype(jnp.float32) + moved).astype(jnp.bfloat16)
    fourth_gradient = (grad_out.astype(jnp.float32) + moved_back).astype(jnp.bfloat16)
    third_gradient, gradient_kernel_second = temporal_backward(
        fourth_gradient,
        fourth_preactivation,
        third_padded,
        second_time_kernel,
        wide_dilation,
    )
    frames_grad_two, grad_sb = spatial_backward(
        third_gradient, pre_three, padded_two, spatial_b, chart_rim
    )
    first_gradient, gradient_kernel_first = temporal_backward(
        frames_grad_two,
        second_preactivation,
        first_padded,
        first_time_kernel,
        NEAR_DILATION,
    )
    grad_features, grad_sa = spatial_backward(
        first_gradient, pre_one, padded_zero, spatial_a, chart_rim
    )
    pixel_frames = total_frames * strips * lax.axis_size("chart") * features.shape[3]
    grad_scale = float(pixel_frames) ** (-0.5)
    summed_sa, summed_ta, summed_sb, summed_tb = exchange_sum(
        (grad_sa, gradient_kernel_first, grad_sb, gradient_kernel_second),
        ("frame", "chart"),
        grad_scale,
    )
    return (
        blended,
        grad_features,
        summed_sa,
        summed_ta,
        summed_sb,
        summed_tb,
    )


def solution(mesh):
    placed = (
        P("frame", "chart", None, None),
        P(),
        P(),
        P(),
        P(),
        P(),
        P(),
        P(),
        P("frame", "chart", None, None),
    )
    return jax.shard_map(
        shards,
        mesh=mesh,
        in_specs=placed,
        out_specs=(
            P("frame", "chart", None, None),
            P("frame", "chart", None, None),
            P(),
            P(),
            P(),
            P(),
        ),
        check_vma=False,
    )
```

```python
import jax
import jax.numpy as jnp
from jax import lax
from jax.sharding import PartitionSpec as P

NEAR_DILATION = 1
REACH = 2
SEAM_CAP = 4


def with_halo(cells, sides, width):
    for axis, dim in sides:
        count = lax.axis_size(axis)
        ends = count - 1
        head = lax.slice_in_dim(cells, 0, width, axis=dim)
        tail = lax.slice_in_dim(cells, cells.shape[dim] - width, cells.shape[dim], axis=dim)
        cells = jnp.concatenate(
            [
                lax.ppermute(tail, axis, [(i, (i + 1) % count) for i in range(ends)]),
                cells,
                lax.ppermute(head, axis, [((i + 1) % count, i) for i in range(ends)]),
            ],
            axis=dim,
        )
    return cells


def from_behind(array, axis, by):
    peers = lax.axis_size(axis)
    pairs = [(i, i + by) for i in range(peers) if 0 <= i + by < peers]
    return lax.ppermute(array, axis, pairs)


def silu_slope(values):
    logistic = jax.nn.sigmoid(values)
    return logistic * (1.0 + values * (1.0 - logistic))


def pad_columns(values):
    return jnp.pad(values, ((0, 0), (0, 0), (0, 0), (1, 1)))


def chart_rim(values):
    return with_halo(values, (("chart", 1),), 1)


def near_send(values, steps_by):
    return from_behind(values, "chart", steps_by)


def spatial_apply(padded, weight):
    strips = padded.shape[1] - 2
    pixels = padded.shape[3] - 2
    summed = None
    for row_tap in range(3):
        for col_tap in range(3):
            partial_sum = jnp.einsum(
                "oc,fscp->fsop",
                weight[row_tap, col_tap],
                padded[:, row_tap : row_tap + strips, :, col_tap : col_tap + pixels],
                preferred_element_type=jnp.float32,
            )
            summed = partial_sum if summed is None else summed + partial_sum
    return summed


def spatial_transpose(padded, weight):
    strips = padded.shape[1] - 2
    pixels = padded.shape[3] - 2
    summed = None
    for row_tap in range(3):
        for col_tap in range(3):
            partial_sum = jnp.einsum(
                "oc,fsop->fscp",
                weight[row_tap, col_tap],
                padded[
                    :, 2 - row_tap : 2 - row_tap + strips, :, 2 - col_tap : 2 - col_tap + pixels
                ],
                preferred_element_type=jnp.float32,
            )
            summed = partial_sum if summed is None else summed + partial_sum
    return summed


def spatial_weight(slopes, padded):
    gathered = lax.conv_general_dilated(
        padded,
        slopes,
        window_strides=(1, 1),
        padding="VALID",
        dimension_numbers=("CHNW", "IHOW", "HWCN"),
        preferred_element_type=jnp.float32,
    )
    return gathered


def spatial_forward(inputs, weight, rim_fn):
    padded = pad_columns(rim_fn(inputs))
    before = spatial_apply(padded, weight)
    output = (inputs.astype(jnp.float32) + jax.nn.silu(before)).astype(jnp.bfloat16)
    return (output, before, padded)


def spatial_backward(upstream, before, padded, weight, rim_fn):
    slopes = (upstream.astype(jnp.float32) * silu_slope(before)).astype(jnp.bfloat16)
    grad_weight = spatial_weight(slopes, padded)
    spread = pad_columns(rim_fn(slopes))
    result = (upstream.astype(jnp.float32) + spatial_transpose(spread, weight)).astype(jnp.bfloat16)
    return (result, grad_weight)


def frame_shift(values, offset):
    count = values.shape[0]
    groups = []
    for frame in range(count):
        peer, row = divmod(frame + offset, count)
        if groups and groups[-1][0] == peer:
            groups[-1][2] = row + 1
        else:
            groups.append([peer, row, row + 1])
    pieces = []
    for peer, first, last in groups:
        piece = values[first:last]
        if peer != 0:
            piece = from_behind(piece, "frame", -peer)
        pieces.append(piece)
    return pieces[0] if len(pieces) == 1 else jnp.concatenate(pieces, axis=0)


def time_taps(values, spacing):
    return (frame_shift(values, -spacing), values, frame_shift(values, spacing))


def time_kernel_forward(inputs, weight, spacing):
    taps = time_taps(inputs, spacing)
    before = None
    for kernel_tap in range(3):
        partial_sum = jnp.einsum(
            "oc,fscp->fsop", weight[kernel_tap], taps[kernel_tap], preferred_element_type=jnp.float32
        )
        before = partial_sum if before is None else before + partial_sum
    output = (inputs.astype(jnp.float32) + jax.nn.silu(before)).astype(jnp.bfloat16)
    return (output, before, taps)


def temporal_backward(upstream, before, taps, weight, spacing):
    slopes = (upstream.astype(jnp.float32) * silu_slope(before)).astype(jnp.bfloat16)
    grad_weight = jnp.stack(
        [
            jnp.einsum("fsop,fscp->oc", slopes, taps[kernel_tap], preferred_element_type=jnp.float32)
            for kernel_tap in range(3)
        ]
    )
    spread = time_taps(slopes, spacing)
    summed = upstream.astype(jnp.float32)
    for kernel_tap in range(3):
        summed = summed + jnp.einsum(
            "oc,fsop->fscp",
            weight[kernel_tap],
            spread[2 - kernel_tap],
            preferred_element_type=jnp.float32,
        )
    return (summed.astype(jnp.bfloat16), grad_weight)


def seam_tables(seam_owner, seam_row, seam_to, strips):
    slot_count = seam_owner.shape[1]
    active = seam_owner >= 0
    earlier = jnp.arange(slot_count)[None, :] < jnp.arange(slot_count)[:, None]
    ordinal = jnp.sum((seam_owner[:, :, None] == seam_owner[:, None, :]) & earlier[None], axis=2)
    myself = lax.axis_index("chart")
    rank_hit = (ordinal[:, None, :] == jnp.arange(SEAM_CAP)[None, :, None]) & active[:, None, :]
    as_owner = rank_hit & (seam_owner[:, None, :] == myself)
    send_strip = jnp.sum(jnp.where(as_owner, seam_row[:, None, :], 0), axis=2)
    send_active = jnp.any(as_owner, axis=2)
    own_owner = lax.dynamic_index_in_dim(seam_owner, myself, 0, keepdims=False)
    own_to = lax.dynamic_index_in_dim(seam_to, myself, 0, keepdims=False)
    own_ordinal = lax.dynamic_index_in_dim(ordinal, myself, 0, keepdims=False)
    landing = (own_to[:, None] == jnp.arange(strips)[None, :]).astype(jnp.float32)
    return (send_strip, send_active, own_owner, own_to, own_ordinal, landing)


def receiver_side(tables, owner_ids):
    own_owner, own_to, own_ordinal, landing = (tables[2], tables[3], tables[4], tables[5])
    match_slot = (
        (own_owner[:, None, None] >= 0)
        & (own_owner[:, None, None] == owner_ids[None, :, None])
        & (own_ordinal[:, None, None] == jnp.arange(SEAM_CAP)[None, None, :])
    )
    matrix = jnp.einsum("kt,kqr->tqr", landing, match_slot.astype(jnp.float32))
    back_strip = jnp.sum(jnp.where(match_slot, own_to[:, None, None], 0), axis=0)
    return (matrix, back_strip)


def sender_side(tables, receiver_ids, strips):
    send_strip, send_active = (tables[0], tables[1])
    tile_count = send_strip.shape[0]
    inside_range = (receiver_ids >= 0) & (receiver_ids < tile_count)
    clipped = jnp.clip(receiver_ids, 0, tile_count - 1)
    strip_ids = jnp.take(send_strip, clipped, axis=0)
    live_ids = jnp.take(send_active, clipped, axis=0) & inside_range[:, None]
    matrix = ((strip_ids[None] == jnp.arange(strips)[:, None, None]) & live_ids[None]).astype(
        jnp.float32
    )
    return (strip_ids, matrix)


def pick_strips(values, strip_ids):
    hot = (strip_ids.reshape(-1)[:, None] == jnp.arange(values.shape[1])[None, :]).astype(
        values.dtype
    )
    gathered = jnp.einsum(
        "qs,fscp->fqcp", hot, values, preferred_element_type=jnp.float32
    ).astype(values.dtype)
    return gathered.reshape(
        values.shape[0], strip_ids.shape[0], strip_ids.shape[1], values.shape[2], values.shape[3]
    )


def place_strips(received, matrix):
    return jnp.einsum(
        "tqr,fqrcp->ftcp", matrix.astype(jnp.bfloat16), received, preferred_element_type=jnp.float32
    )


def exchange_sum(parts, axes):
    flat = jnp.concatenate([part.reshape(-1) for part in parts])
    size = 1
    for axis in axes:
        size *= lax.axis_size(axis)
    pieces = flat.reshape(size, -1)
    flat = jnp.sum(lax.all_to_all(pieces, axes, 0, 0, tiled=True), axis=0)
    copies = jnp.broadcast_to(flat[None], (size,) + flat.shape)
    flat = lax.all_to_all(copies, axes, 0, 0, tiled=True).reshape(-1)
    results = []
    start = 0
    for part in parts:
        results.append(flat[start : start + part.size].reshape(part.shape))
        start += part.size
    return results


def shards(
    features,
    spatial_a,
    first_time_kernel,
    spatial_b,
    second_time_kernel,
    seam_owner,
    seam_row,
    seam_to,
    grad_out,
):
    total_frames = features.shape[0] * lax.axis_size("frame")
    wide_dilation = min(8, total_frames // 4)
    strips = features.shape[1]
    first_layer, pre_one, padded_zero = spatial_forward(features, spatial_a, chart_rim)
    second_layer, second_preactivation, first_padded = time_kernel_forward(
        first_layer, first_time_kernel, NEAR_DILATION
    )
    frames_three, pre_three, padded_two = spatial_forward(second_layer, spatial_b, chart_rim)
    frames_four, fourth_preactivation, third_padded = time_kernel_forward(
        frames_three, second_time_kernel, wide_dilation
    )
    tables = seam_tables(seam_owner, seam_row, seam_to, strips)
    myself = lax.axis_index("chart")
    offsets = [offset for offset in range(-REACH, REACH + 1) if offset != 0]
    offset_array = jnp.array(offsets, dtype=jnp.int32)
    receive_matrix, back_strip = receiver_side(tables, myself + offset_array)
    outgoing = {}
    for position, offset in enumerate(offsets):
        strip_ids, unused_matrix = sender_side(tables, jnp.reshape(myself - offset, (1,)), strips)
        outgoing[offset] = pick_strips(frames_four, strip_ids)
    arrivals = {}
    returns = {}
    for position, offset in enumerate(offsets):
        going_back = pick_strips(grad_out, back_strip[position : position + 1])
        payload = jnp.concatenate([outgoing[-offset], going_back], axis=1)
        landed = near_send(payload, offset)
        arrivals[-offset] = landed[:, :1]
        returns[offset] = landed[:, 1:]
    moved = place_strips(
        jnp.concatenate([arrivals[offset] for offset in offsets], axis=1), receive_matrix
    )
    unused_ids, return_matrix = sender_side(tables, myself - offset_array, strips)
    moved_back = place_strips(
        jnp.concatenate([returns[offset] for offset in offsets], axis=1), return_matrix
    )
    blended = (frames_four.astype(jnp.float32) + moved).astype(jnp.bfloat16)
    fourth_gradient = (grad_out.astype(jnp.float32) + moved_back).astype(jnp.bfloat16)
    third_gradient, gradient_kernel_second = temporal_backward(
        fourth_gradient,
        fourth_preactivation,
        third_padded,
        second_time_kernel,
        wide_dilation,
    )
    frames_grad_two, grad_sb = spatial_backward(
        third_gradient, pre_three, padded_two, spatial_b, chart_rim
    )
    first_gradient, gradient_kernel_first = temporal_backward(
        frames_grad_two,
        second_preactivation,
        first_padded,
        first_time_kernel,
        NEAR_DILATION,
    )
    grad_features, grad_sa = spatial_backward(
        first_gradient, pre_one, padded_zero, spatial_a, chart_rim
    )
    summed_sa, summed_ta, summed_sb, summed_tb = exchange_sum(
        (grad_sa, gradient_kernel_first, grad_sb, gradient_kernel_second), ("frame", "chart")
    )
    pixel_frames = total_frames * strips * lax.axis_size("chart") * features.shape[3]
    grad_scale = float(pixel_frames) ** (-0.5)
    return (
        blended,
        grad_features,
        summed_sa * grad_scale,
        summed_ta * grad_scale,
        summed_sb * grad_scale,
        summed_tb * grad_scale,
    )


def solution(mesh):
    placed = (
        P("frame", "chart", None, None),
        P(),
        P(),
        P(),
        P(),
        P(),
        P(),
        P(),
        P("frame", "chart", None, None),
    )
    return jax.shard_map(
        shards,
        mesh=mesh,
        in_specs=placed,
        out_specs=(
            P("frame", "chart", None, None),
            P("frame", "chart", None, None),
            P(),
            P(),
            P(),
            P(),
        ),
        check_vma=False,
    )
```

```python
import jax
import jax.numpy as jnp
from jax import lax
from jax.sharding import PartitionSpec as P

NEAR_DILATION = 1
REACH = 2
SEAM_CAP = 4


def with_halo(cells, sides, width):
    for axis, dim in sides:
        count = lax.axis_size(axis)
        ends = count - 1
        head = lax.slice_in_dim(cells, 0, width, axis=dim)
        tail = lax.slice_in_dim(cells, cells.shape[dim] - width, cells.shape[dim], axis=dim)
        cells = jnp.concatenate(
            [
                lax.ppermute(tail, axis, [(i, (i + 1) % count) for i in range(ends)]),
                cells,
                lax.ppermute(head, axis, [((i + 1) % count, i) for i in range(ends)]),
            ],
            axis=dim,
        )
    return cells


def from_behind(array, axis, by):
    peers = lax.axis_size(axis)
    pairs = [(i, i + by) for i in range(peers) if 0 <= i + by < peers]
    return lax.ppermute(array, axis, pairs)


def silu_slope(values):
    logistic = jax.nn.sigmoid(values)
    return logistic * (1.0 + values * (1.0 - logistic))


def pad_columns(values):
    return jnp.pad(values, ((0, 0), (0, 0), (0, 0), (1, 1)))


def chart_rim(values):
    return with_halo(values, (("chart", 1),), 1)


def rim_with_riders(riders, landed):
    def rim(values):
        head = values[:, :1]
        tail = values[:, -1:]
        plus, minus = riders
        shape = plus.shape
        flat_shape = (shape[0], shape[1] * shape[2]) + shape[3:]
        up = near_send(jnp.concatenate([tail, plus.reshape(flat_shape)], axis=1), 1)
        down = near_send(jnp.concatenate([head, minus.reshape(flat_shape)], axis=1), -1)
        landed[1] = up[:, 1:].reshape(shape)
        landed[-1] = down[:, 1:].reshape(shape)
        return jnp.concatenate([up[:, :1], values, down[:, :1]], axis=1)

    return rim


def near_send(values, steps_by):
    return from_behind(values, "chart", steps_by)


def spatial_apply(padded, weight):
    strips = padded.shape[1] - 2
    pixels = padded.shape[3] - 2
    summed = None
    for row_tap in range(3):
        for col_tap in range(3):
            partial_sum = jnp.einsum(
                "oc,fscp->fsop",
                weight[row_tap, col_tap],
                padded[:, row_tap : row_tap + strips, :, col_tap : col_tap + pixels],
                preferred_element_type=jnp.float32,
            )
            summed = partial_sum if summed is None else summed + partial_sum
    return summed


def spatial_transpose(padded, weight):
    strips = padded.shape[1] - 2
    pixels = padded.shape[3] - 2
    summed = None
    for row_tap in range(3):
        for col_tap in range(3):
            partial_sum = jnp.einsum(
                "oc,fsop->fscp",
                weight[row_tap, col_tap],
                padded[
                    :, 2 - row_tap : 2 - row_tap + strips, :, 2 - col_tap : 2 - col_tap + pixels
                ],
                preferred_element_type=jnp.float32,
            )
            summed = partial_sum if summed is None else summed + partial_sum
    return summed


def spatial_weight(slopes, padded):
    strips = slopes.shape[1]
    pixels = slopes.shape[3]
    return jnp.stack(
        [
            jnp.stack(
                [
                    jnp.einsum(
                        "fsop,fscp->oc",
                        slopes,
                        padded[:, row_tap : row_tap + strips, :, col_tap : col_tap + pixels],
                        preferred_element_type=jnp.float32,
                    )
                    for col_tap in range(3)
                ]
            )
            for row_tap in range(3)
        ]
    )


def spatial_forward(inputs, weight, rim_fn):
    padded = pad_columns(rim_fn(inputs))
    before = spatial_apply(padded, weight)
    output = (inputs.astype(jnp.float32) + jax.nn.silu(before)).astype(jnp.bfloat16)
    return (output, before, padded)


def spatial_backward(upstream, before, padded, weight, rim_fn):
    slopes = (upstream.astype(jnp.float32) * silu_slope(before)).astype(jnp.bfloat16)
    grad_weight = spatial_weight(slopes, padded)
    spread = pad_columns(rim_fn(slopes))
    result = (upstream.astype(jnp.float32) + spatial_transpose(spread, weight)).astype(jnp.bfloat16)
    return (result, grad_weight)


def frame_shift(values, offset):
    count = values.shape[0]
    groups = []
    for frame in range(count):
        peer, row = divmod(frame + offset, count)
        if groups and groups[-1][0] == peer:
            groups[-1][2] = row + 1
        else:
            groups.append([peer, row, row + 1])
    pieces = []
    for peer, first, last in groups:
        piece = values[first:last]
        if peer != 0:
            piece = from_behind(piece, "frame", -peer)
        pieces.append(piece)
    return pieces[0] if len(pieces) == 1 else jnp.concatenate(pieces, axis=0)


def time_taps(values, spacing):
    return (frame_shift(values, -spacing), values, frame_shift(values, spacing))


def time_kernel_forward(inputs, weight, spacing):
    taps = time_taps(inputs, spacing)
    before = None
    for kernel_tap in range(3):
        partial_sum = jnp.einsum(
            "oc,fscp->fsop", weight[kernel_tap], taps[kernel_tap], preferred_element_type=jnp.float32
        )
        before = partial_sum if before is None else before + partial_sum
    output = (inputs.astype(jnp.float32) + jax.nn.silu(before)).astype(jnp.bfloat16)
    return (output, before, taps)


def temporal_backward(upstream, before, taps, weight, spacing):
    slopes = (upstream.astype(jnp.float32) * silu_slope(before)).astype(jnp.bfloat16)
    grad_weight = jnp.stack(
        [
            jnp.einsum("fsop,fscp->oc", slopes, taps[kernel_tap], preferred_element_type=jnp.float32)
            for kernel_tap in range(3)
        ]
    )
    spread = time_taps(slopes, spacing)
    summed = upstream.astype(jnp.float32)
    for kernel_tap in range(3):
        summed = summed + jnp.einsum(
            "oc,fsop->fscp",
            weight[kernel_tap],
            spread[2 - kernel_tap],
            preferred_element_type=jnp.float32,
        )
    return (summed.astype(jnp.bfloat16), grad_weight)


def seam_tables(seam_owner, seam_row, seam_to, strips):
    slot_count = seam_owner.shape[1]
    active = seam_owner >= 0
    earlier = jnp.arange(slot_count)[None, :] < jnp.arange(slot_count)[:, None]
    ordinal = jnp.sum((seam_owner[:, :, None] == seam_owner[:, None, :]) & earlier[None], axis=2)
    myself = lax.axis_index("chart")
    rank_hit = (ordinal[:, None, :] == jnp.arange(SEAM_CAP)[None, :, None]) & active[:, None, :]
    as_owner = rank_hit & (seam_owner[:, None, :] == myself)
    send_strip = jnp.sum(jnp.where(as_owner, seam_row[:, None, :], 0), axis=2)
    send_active = jnp.any(as_owner, axis=2)
    own_owner = lax.dynamic_index_in_dim(seam_owner, myself, 0, keepdims=False)
    own_to = lax.dynamic_index_in_dim(seam_to, myself, 0, keepdims=False)
    own_ordinal = lax.dynamic_index_in_dim(ordinal, myself, 0, keepdims=False)
    landing = (own_to[:, None] == jnp.arange(strips)[None, :]).astype(jnp.float32)
    return (send_strip, send_active, own_owner, own_to, own_ordinal, landing)


def receiver_side(tables, owner_ids):
    own_owner, own_to, own_ordinal, landing = (tables[2], tables[3], tables[4], tables[5])
    match_slot = (
        (own_owner[:, None, None] >= 0)
        & (own_owner[:, None, None] == owner_ids[None, :, None])
        & (own_ordinal[:, None, None] == jnp.arange(SEAM_CAP)[None, None, :])
    )
    matrix = jnp.einsum("kt,kqr->tqr", landing, match_slot.astype(jnp.float32))
    back_strip = jnp.sum(jnp.where(match_slot, own_to[:, None, None], 0), axis=0)
    return (matrix, back_strip)


def sender_side(tables, receiver_ids, strips):
    send_strip, send_active = (tables[0], tables[1])
    tile_count = send_strip.shape[0]
    inside_range = (receiver_ids >= 0) & (receiver_ids < tile_count)
    clipped = jnp.clip(receiver_ids, 0, tile_count - 1)
    strip_ids = jnp.take(send_strip, clipped, axis=0)
    live_ids = jnp.take(send_active, clipped, axis=0) & inside_range[:, None]
    matrix = ((strip_ids[None] == jnp.arange(strips)[:, None, None]) & live_ids[None]).astype(
        jnp.float32
    )
    return (strip_ids, matrix)


def pick_strips(values, strip_ids):
    hot = (strip_ids.reshape(-1)[:, None] == jnp.arange(values.shape[1])[None, :]).astype(
        values.dtype
    )
    gathered = jnp.einsum(
        "qs,fscp->fqcp", hot, values, preferred_element_type=jnp.float32
    ).astype(values.dtype)
    return gathered.reshape(
        values.shape[0], strip_ids.shape[0], strip_ids.shape[1], values.shape[2], values.shape[3]
    )


def place_strips(received, matrix):
    return jnp.einsum(
        "tqr,fqrcp->ftcp", matrix.astype(jnp.bfloat16), received, preferred_element_type=jnp.float32
    )


def exchange_sum(parts, axes):
    flat = jnp.concatenate([part.reshape(-1) for part in parts])
    size = 1
    for axis in axes:
        size *= lax.axis_size(axis)
    pieces = flat.reshape(size, -1)
    flat = jnp.sum(lax.all_to_all(pieces, axes, 0, 0, tiled=True), axis=0)
    copies = jnp.broadcast_to(flat[None], (size,) + flat.shape)
    flat = lax.all_to_all(copies, axes, 0, 0, tiled=True).reshape(-1)
    results = []
    start = 0
    for part in parts:
        results.append(flat[start : start + part.size].reshape(part.shape))
        start += part.size
    return results


def shards(
    features,
    spatial_a,
    first_time_kernel,
    spatial_b,
    second_time_kernel,
    seam_owner,
    seam_row,
    seam_to,
    grad_out,
):
    total_frames = features.shape[0] * lax.axis_size("frame")
    wide_dilation = min(8, total_frames // 4)
    strips = features.shape[1]
    tables = seam_tables(seam_owner, seam_row, seam_to, strips)
    myself = lax.axis_index("chart")
    offsets = [offset for offset in range(-REACH, REACH + 1) if offset != 0]
    offset_array = jnp.array(offsets, dtype=jnp.int32)
    receive_matrix, back_strip = receiver_side(tables, myself + offset_array)
    going_back = {}
    for position, offset in enumerate(offsets):
        going_back[offset] = pick_strips(grad_out, back_strip[position : position + 1])
    returns = {}
    first_layer, pre_one, padded_zero = spatial_forward(
        features, spatial_a, rim_with_riders((going_back[1], going_back[-1]), returns)
    )
    second_layer, second_preactivation, first_padded = time_kernel_forward(
        first_layer, first_time_kernel, NEAR_DILATION
    )
    frames_three, pre_three, padded_two = spatial_forward(second_layer, spatial_b, chart_rim)
    frames_four, fourth_preactivation, third_padded = time_kernel_forward(
        frames_three, second_time_kernel, wide_dilation
    )
    outgoing = {}
    for position, offset in enumerate(offsets):
        strip_ids, unused_matrix = sender_side(tables, jnp.reshape(myself - offset, (1,)), strips)
        outgoing[offset] = pick_strips(frames_four, strip_ids)
    arrivals = {}
    for offset in offsets:
        if abs(offset) == 1:
            continue
        payload = jnp.concatenate([outgoing[-offset], going_back[offset]], axis=1)
        landed = near_send(payload, offset)
        arrivals[-offset] = landed[:, :1]
        returns[offset] = landed[:, 1:]
    unused_ids, return_matrix = sender_side(tables, myself - offset_array, strips)
    moved_back = place_strips(
        jnp.concatenate([returns[offset] for offset in offsets], axis=1), return_matrix
    )
    fourth_gradient = (grad_out.astype(jnp.float32) + moved_back).astype(jnp.bfloat16)
    third_gradient, gradient_kernel_second = temporal_backward(
        fourth_gradient,
        fourth_preactivation,
        third_padded,
        second_time_kernel,
        wide_dilation,
    )
    carried = {}
    frames_grad_two, grad_sb = spatial_backward(
        third_gradient,
        pre_three,
        padded_two,
        spatial_b,
        rim_with_riders((outgoing[-1], outgoing[1]), carried),
    )
    arrivals[-1] = carried[1]
    arrivals[1] = carried[-1]
    moved = place_strips(
        jnp.concatenate([arrivals[offset] for offset in offsets], axis=1), receive_matrix
    )
    blended = (frames_four.astype(jnp.float32) + moved).astype(jnp.bfloat16)
    first_gradient, gradient_kernel_first = temporal_backward(
        frames_grad_two,
        second_preactivation,
        first_padded,
        first_time_kernel,
        NEAR_DILATION,
    )
    grad_features, grad_sa = spatial_backward(
        first_gradient, pre_one, padded_zero, spatial_a, chart_rim
    )
    summed_sa, summed_ta, summed_sb, summed_tb = exchange_sum(
        (grad_sa, gradient_kernel_first, grad_sb, gradient_kernel_second), ("frame", "chart")
    )
    pixel_frames = total_frames * strips * lax.axis_size("chart") * features.shape[3]
    grad_scale = float(pixel_frames) ** (-0.5)
    return (
        blended,
        grad_features,
        summed_sa * grad_scale,
        summed_ta * grad_scale,
        summed_sb * grad_scale,
        summed_tb * grad_scale,
    )


def solution(mesh):
    placed = (
        P("frame", "chart", None, None),
        P(),
        P(),
        P(),
        P(),
        P(),
        P(),
        P(),
        P("frame", "chart", None, None),
    )
    return jax.shard_map(
        shards,
        mesh=mesh,
        in_specs=placed,
        out_specs=(
            P("frame", "chart", None, None),
            P("frame", "chart", None, None),
            P(),
            P(),
            P(),
            P(),
        ),
        check_vma=False,
    )
```

```python
import jax
import jax.numpy as jnp
from jax import lax
from jax.sharding import PartitionSpec as P

NEAR_DILATION = 1
REACH = 2
SEAM_CAP = 4


def with_halo(cells, sides, width):
    for axis, dim in sides:
        count = lax.axis_size(axis)
        ends = count - 1
        head = lax.slice_in_dim(cells, 0, width, axis=dim)
        tail = lax.slice_in_dim(cells, cells.shape[dim] - width, cells.shape[dim], axis=dim)
        cells = jnp.concatenate(
            [
                lax.ppermute(tail, axis, [(i, (i + 1) % count) for i in range(ends)]),
                cells,
                lax.ppermute(head, axis, [((i + 1) % count, i) for i in range(ends)]),
            ],
            axis=dim,
        )
    return cells


def from_behind(array, axis, by):
    peers = lax.axis_size(axis)
    pairs = [(i, i + by) for i in range(peers) if 0 <= i + by < peers]
    return lax.ppermute(array, axis, pairs)


def silu_slope(values):
    logistic = jax.nn.sigmoid(values)
    return logistic * (1.0 + values * (1.0 - logistic))


def pad_columns(values):
    return jnp.pad(values, ((0, 0), (0, 0), (0, 0), (1, 1)))


def chart_rim(values):
    return with_halo(values, (("chart", 1),), 1)


def near_send(values, steps_by):
    return from_behind(values, "chart", steps_by)


def spatial_apply(padded, weight):
    strips = padded.shape[1] - 2
    pixels = padded.shape[3] - 2
    summed = None
    for row_tap in range(3):
        for col_tap in range(3):
            partial_sum = jnp.einsum(
                "oc,fscp->fsop",
                weight[row_tap, col_tap],
                padded[:, row_tap : row_tap + strips, :, col_tap : col_tap + pixels],
                preferred_element_type=jnp.float32,
            )
            summed = partial_sum if summed is None else summed + partial_sum
    return summed


def spatial_transpose(padded, weight):
    strips = padded.shape[1] - 2
    pixels = padded.shape[3] - 2
    summed = None
    for row_tap in range(3):
        for col_tap in range(3):
            partial_sum = jnp.einsum(
                "oc,fsop->fscp",
                weight[row_tap, col_tap],
                padded[
                    :, 2 - row_tap : 2 - row_tap + strips, :, 2 - col_tap : 2 - col_tap + pixels
                ],
                preferred_element_type=jnp.float32,
            )
            summed = partial_sum if summed is None else summed + partial_sum
    return summed


def spatial_weight(slopes, padded):
    strips = slopes.shape[1]
    pixels = slopes.shape[3]
    return jnp.stack(
        [
            jnp.stack(
                [
                    jnp.einsum(
                        "fsop,fscp->oc",
                        slopes,
                        padded[:, row_tap : row_tap + strips, :, col_tap : col_tap + pixels],
                        preferred_element_type=jnp.float32,
                    )
                    for col_tap in range(3)
                ]
            )
            for row_tap in range(3)
        ]
    )


def spatial_forward(inputs, weight, rim_fn):
    padded = pad_columns(rim_fn(inputs))
    before = spatial_apply(padded, weight)
    output = (inputs.astype(jnp.float32) + jax.nn.silu(before)).astype(jnp.bfloat16)
    return (output, before, padded)


def spatial_backward(upstream, before, padded, weight, rim_fn):
    slopes = (upstream.astype(jnp.float32) * silu_slope(before)).astype(jnp.bfloat16)
    grad_weight = spatial_weight(slopes, padded)
    spread = pad_columns(rim_fn(slopes))
    result = (upstream.astype(jnp.float32) + spatial_transpose(spread, weight)).astype(jnp.bfloat16)
    return (result, grad_weight)


def frame_shift(values, offset):
    count = values.shape[0]
    groups = []
    for frame in range(count):
        peer, row = divmod(frame + offset, count)
        if groups and groups[-1][0] == peer:
            groups[-1][2] = row + 1
        else:
            groups.append([peer, row, row + 1])
    pieces = []
    for peer, first, last in groups:
        piece = values[first:last]
        if peer != 0:
            piece = from_behind(piece, "frame", -peer)
        pieces.append(piece)
    return pieces[0] if len(pieces) == 1 else jnp.concatenate(pieces, axis=0)


def time_taps(values, spacing):
    return (frame_shift(values, -spacing), values, frame_shift(values, spacing))


def time_kernel_forward(inputs, weight, spacing):
    taps = time_taps(inputs, spacing)
    before = None
    for kernel_tap in range(3):
        partial_sum = jnp.einsum(
            "oc,fscp->fsop", weight[kernel_tap], taps[kernel_tap], preferred_element_type=jnp.float32
        )
        before = partial_sum if before is None else before + partial_sum
    output = (inputs.astype(jnp.float32) + jax.nn.silu(before)).astype(jnp.bfloat16)
    return (output, before, taps)


def temporal_backward(upstream, before, taps, weight, spacing):
    slopes = (upstream.astype(jnp.float32) * silu_slope(before)).astype(jnp.bfloat16)
    grad_weight = jnp.stack(
        [
            jnp.einsum("fsop,fscp->oc", slopes, taps[kernel_tap], preferred_element_type=jnp.float32)
            for kernel_tap in range(3)
        ]
    )
    spread = time_taps(slopes, spacing)
    summed = upstream.astype(jnp.float32)
    for kernel_tap in range(3):
        summed = summed + jnp.einsum(
            "oc,fsop->fscp",
            weight[kernel_tap],
            spread[2 - kernel_tap],
            preferred_element_type=jnp.float32,
        )
    return (summed.astype(jnp.bfloat16), grad_weight)


def seam_tables(seam_owner, seam_row, seam_to, strips):
    slot_count = seam_owner.shape[1]
    active = seam_owner >= 0
    earlier = jnp.arange(slot_count)[None, :] < jnp.arange(slot_count)[:, None]
    ordinal = jnp.sum((seam_owner[:, :, None] == seam_owner[:, None, :]) & earlier[None], axis=2)
    myself = lax.axis_index("chart")
    rank_hit = (ordinal[:, None, :] == jnp.arange(SEAM_CAP)[None, :, None]) & active[:, None, :]
    as_owner = rank_hit & (seam_owner[:, None, :] == myself)
    send_strip = jnp.sum(jnp.where(as_owner, seam_row[:, None, :], 0), axis=2)
    send_active = jnp.any(as_owner, axis=2)
    own_owner = lax.dynamic_index_in_dim(seam_owner, myself, 0, keepdims=False)
    own_to = lax.dynamic_index_in_dim(seam_to, myself, 0, keepdims=False)
    own_ordinal = lax.dynamic_index_in_dim(ordinal, myself, 0, keepdims=False)
    landing = (own_to[:, None] == jnp.arange(strips)[None, :]).astype(jnp.float32)
    return (send_strip, send_active, own_owner, own_to, own_ordinal, landing)


def receiver_side(tables, owner_ids):
    own_owner, own_to, own_ordinal, landing = (tables[2], tables[3], tables[4], tables[5])
    match_slot = (
        (own_owner[:, None, None] >= 0)
        & (own_owner[:, None, None] == owner_ids[None, :, None])
        & (own_ordinal[:, None, None] == jnp.arange(SEAM_CAP)[None, None, :])
    )
    matrix = jnp.einsum("kt,kqr->tqr", landing, match_slot.astype(jnp.float32))
    back_strip = jnp.sum(jnp.where(match_slot, own_to[:, None, None], 0), axis=0)
    return (matrix, back_strip)


def sender_side(tables, receiver_ids, strips):
    send_strip, send_active = (tables[0], tables[1])
    tile_count = send_strip.shape[0]
    inside_range = (receiver_ids >= 0) & (receiver_ids < tile_count)
    clipped = jnp.clip(receiver_ids, 0, tile_count - 1)
    strip_ids = jnp.take(send_strip, clipped, axis=0)
    live_ids = jnp.take(send_active, clipped, axis=0) & inside_range[:, None]
    matrix = ((strip_ids[None] == jnp.arange(strips)[:, None, None]) & live_ids[None]).astype(
        jnp.float32
    )
    return (strip_ids, matrix)


def pick_strips(values, strip_ids):
    hot = (strip_ids.reshape(-1)[:, None] == jnp.arange(values.shape[1])[None, :]).astype(
        values.dtype
    )
    gathered = jnp.einsum(
        "qs,fscp->fqcp", hot, values, preferred_element_type=jnp.float32
    ).astype(values.dtype)
    return gathered.reshape(
        values.shape[0], strip_ids.shape[0], strip_ids.shape[1], values.shape[2], values.shape[3]
    )


def place_strips(received, matrix):
    return jnp.einsum(
        "tqr,fqrcp->ftcp", matrix.astype(jnp.bfloat16), received, preferred_element_type=jnp.float32
    )


def exchange_sum(parts, axes):
    flat = jnp.concatenate([part.reshape(-1) for part in parts])
    size = 1
    for axis in axes:
        size *= lax.axis_size(axis)
    pieces = flat.reshape(size, -1)
    flat = jnp.sum(lax.all_to_all(pieces, axes, 0, 0, tiled=True), axis=0)
    copies = jnp.broadcast_to(flat[None], (size,) + flat.shape)
    flat = lax.all_to_all(copies, axes, 0, 0, tiled=True).reshape(-1)
    results = []
    start = 0
    for part in parts:
        results.append(flat[start : start + part.size].reshape(part.shape))
        start += part.size
    return results


def shards(
    features,
    spatial_a,
    first_time_kernel,
    spatial_b,
    second_time_kernel,
    seam_owner,
    seam_row,
    seam_to,
    grad_out,
):
    total_frames = features.shape[0] * lax.axis_size("frame")
    wide_dilation = min(8, total_frames // 4)
    strips = features.shape[1]
    first_layer, pre_one, padded_zero = spatial_forward(features, spatial_a, chart_rim)
    second_layer, second_preactivation, first_padded = time_kernel_forward(
        first_layer, first_time_kernel, NEAR_DILATION
    )
    frames_three, pre_three, padded_two = spatial_forward(second_layer, spatial_b, chart_rim)
    frames_four, fourth_preactivation, third_padded = time_kernel_forward(
        frames_three, second_time_kernel, wide_dilation
    )
    tables = seam_tables(seam_owner, seam_row, seam_to, strips)
    myself = lax.axis_index("chart")
    offsets = [offset for offset in range(-REACH, REACH + 1) if offset != 0]
    offset_array = jnp.array(offsets, dtype=jnp.int32)
    receive_matrix, back_strip = receiver_side(tables, myself + offset_array)
    outgoing = {}
    for position, offset in enumerate(offsets):
        strip_ids, unused_matrix = sender_side(tables, jnp.reshape(myself - offset, (1,)), strips)
        outgoing[offset] = pick_strips(frames_four, strip_ids)
    arrivals = {}
    returns = {}
    for position, offset in enumerate(offsets):
        going_back = pick_strips(grad_out, back_strip[position : position + 1])
        payload = jnp.concatenate([outgoing[-offset], going_back], axis=1)
        landed = near_send(payload, offset)
        arrivals[-offset] = landed[:, :1]
        returns[offset] = landed[:, 1:]
    moved = place_strips(
        jnp.concatenate([arrivals[offset] for offset in offsets], axis=1), receive_matrix
    )
    unused_ids, return_matrix = sender_side(tables, myself - offset_array, strips)
    moved_back = place_strips(
        jnp.concatenate([returns[offset] for offset in offsets], axis=1), return_matrix
    )
    blended = (frames_four.astype(jnp.float32) + moved).astype(jnp.bfloat16)
    fourth_gradient = (grad_out.astype(jnp.float32) + moved_back).astype(jnp.bfloat16)
    third_gradient, gradient_kernel_second = temporal_backward(
        fourth_gradient,
        fourth_preactivation,
        third_padded,
        second_time_kernel,
        wide_dilation,
    )
    frames_grad_two, grad_sb = spatial_backward(
        third_gradient, pre_three, padded_two, spatial_b, chart_rim
    )
    first_gradient, gradient_kernel_first = temporal_backward(
        frames_grad_two,
        second_preactivation,
        first_padded,
        first_time_kernel,
        NEAR_DILATION,
    )
    grad_features, grad_sa = spatial_backward(
        first_gradient, pre_one, padded_zero, spatial_a, chart_rim
    )
    summed_sa, summed_ta, summed_sb, summed_tb = exchange_sum(
        (grad_sa, gradient_kernel_first, grad_sb, gradient_kernel_second), ("chart", "frame")
    )
    pixel_frames = total_frames * strips * lax.axis_size("chart") * features.shape[3]
    grad_scale = float(pixel_frames) ** (-0.5)
    return (
        blended,
        grad_features,
        summed_sa * grad_scale,
        summed_ta * grad_scale,
        summed_sb * grad_scale,
        summed_tb * grad_scale,
    )


def solution(mesh):
    placed = (
        P("frame", "chart", None, None),
        P(),
        P(),
        P(),
        P(),
        P(),
        P(),
        P(),
        P("frame", "chart", None, None),
    )
    return jax.shard_map(
        shards,
        mesh=mesh,
        in_specs=placed,
        out_specs=(
            P("frame", "chart", None, None),
            P("frame", "chart", None, None),
            P(),
            P(),
            P(),
            P(),
        ),
        check_vma=False,
    )
```

```python
import jax
import jax.numpy as jnp
from jax import lax
from jax.sharding import PartitionSpec as P

NEAR_DILATION = 1
REACH = 2
SEAM_CAP = 4


def with_halo(cells, sides, width):
    for axis, dim in sides:
        count = lax.axis_size(axis)
        ends = count - 1
        head = lax.slice_in_dim(cells, 0, width, axis=dim)
        tail = lax.slice_in_dim(cells, cells.shape[dim] - width, cells.shape[dim], axis=dim)
        cells = jnp.concatenate(
            [
                lax.ppermute(tail, axis, [(i, (i + 1) % count) for i in range(ends)]),
                cells,
                lax.ppermute(head, axis, [((i + 1) % count, i) for i in range(ends)]),
            ],
            axis=dim,
        )
    return cells


def from_behind(array, axis, by):
    peers = lax.axis_size(axis)
    pairs = [(i, i + by) for i in range(peers) if 0 <= i + by < peers]
    return lax.ppermute(array, axis, pairs)


def silu_slope(values):
    logistic = jax.nn.sigmoid(values)
    return logistic * (1.0 + values * (1.0 - logistic))


def pad_columns(values):
    return jnp.pad(values, ((0, 0), (0, 0), (0, 0), (1, 1)))


def chart_rim(values):
    return with_halo(values, (("chart", 1),), 1)


def near_send(values, steps_by):
    return from_behind(values, "chart", steps_by)


def spatial_apply(padded, weight):
    strips = padded.shape[1] - 2
    pixels = padded.shape[3] - 2
    summed = None
    for row_tap in range(3):
        for col_tap in range(3):
            partial_sum = jnp.einsum(
                "oc,fscp->fsop",
                weight[row_tap, col_tap],
                padded[:, row_tap : row_tap + strips, :, col_tap : col_tap + pixels],
                preferred_element_type=jnp.float32,
            )
            summed = partial_sum if summed is None else summed + partial_sum
    return summed


def spatial_transpose(padded, weight):
    strips = padded.shape[1] - 2
    pixels = padded.shape[3] - 2
    summed = None
    for row_tap in range(3):
        for col_tap in range(3):
            partial_sum = jnp.einsum(
                "oc,fsop->fscp",
                weight[row_tap, col_tap],
                padded[
                    :, 2 - row_tap : 2 - row_tap + strips, :, 2 - col_tap : 2 - col_tap + pixels
                ],
                preferred_element_type=jnp.float32,
            )
            summed = partial_sum if summed is None else summed + partial_sum
    return summed


def spatial_weight(slopes, padded):
    strips = slopes.shape[1]
    pixels = slopes.shape[3]
    return jnp.stack(
        [
            jnp.stack(
                [
                    jnp.einsum(
                        "fsop,fscp->oc",
                        slopes,
                        padded[:, row_tap : row_tap + strips, :, col_tap : col_tap + pixels],
                        preferred_element_type=jnp.float32,
                    )
                    for col_tap in range(3)
                ]
            )
            for row_tap in range(3)
        ]
    )


def spatial_forward(inputs, weight, rim_fn):
    padded = pad_columns(rim_fn(inputs))
    before = spatial_apply(padded, weight)
    output = (inputs.astype(jnp.float32) + jax.nn.silu(before)).astype(jnp.bfloat16)
    return (output, before, padded)


def spatial_backward(upstream, before, padded, weight, rim_fn):
    slopes = (upstream.astype(jnp.float32) * silu_slope(before)).astype(jnp.bfloat16)
    grad_weight = spatial_weight(slopes, padded)
    spread = pad_columns(rim_fn(slopes))
    result = (upstream.astype(jnp.float32) + spatial_transpose(spread, weight)).astype(jnp.bfloat16)
    return (result, grad_weight)


def frame_shift(values, offset):
    count = values.shape[0]
    groups = []
    for frame in range(count):
        peer, row = divmod(frame + offset, count)
        if groups and groups[-1][0] == peer:
            groups[-1][2] = row + 1
        else:
            groups.append([peer, row, row + 1])
    pieces = []
    for peer, first, last in groups:
        piece = values[first:last]
        if peer != 0:
            piece = from_behind(piece, "frame", -peer)
        pieces.append(piece)
    return pieces[0] if len(pieces) == 1 else jnp.concatenate(pieces, axis=0)


def time_taps(values, spacing):
    return (frame_shift(values, -spacing), values, frame_shift(values, spacing))


def time_kernel_forward(inputs, weight, spacing):
    taps = time_taps(inputs, spacing)
    before = None
    for kernel_tap in range(3):
        partial_sum = jnp.einsum(
            "oc,fscp->fsop", weight[kernel_tap], taps[kernel_tap], preferred_element_type=jnp.float32
        )
        before = partial_sum if before is None else before + partial_sum
    output = (inputs.astype(jnp.float32) + jax.nn.silu(before)).astype(jnp.bfloat16)
    return (output, before, taps)


def temporal_backward(upstream, before, taps, weight, spacing):
    slopes = (upstream.astype(jnp.float32) * silu_slope(before)).astype(jnp.bfloat16)
    grad_weight = jnp.stack(
        [
            jnp.einsum("fsop,fscp->oc", slopes, taps[kernel_tap], preferred_element_type=jnp.float32)
            for kernel_tap in range(3)
        ]
    )
    spread = time_taps(slopes, spacing)
    summed = upstream.astype(jnp.float32)
    for kernel_tap in range(3):
        summed = summed + jnp.einsum(
            "oc,fsop->fscp",
            weight[kernel_tap],
            spread[2 - kernel_tap],
            preferred_element_type=jnp.float32,
        )
    return (summed.astype(jnp.bfloat16), grad_weight)


def seam_tables(seam_owner, seam_row, seam_to, strips):
    slot_count = seam_owner.shape[1]
    active = seam_owner >= 0
    earlier = jnp.arange(slot_count)[None, :] < jnp.arange(slot_count)[:, None]
    ordinal = jnp.sum((seam_owner[:, :, None] == seam_owner[:, None, :]) & earlier[None], axis=2)
    myself = lax.axis_index("chart")
    rank_hit = (ordinal[:, None, :] == jnp.arange(SEAM_CAP)[None, :, None]) & active[:, None, :]
    as_owner = rank_hit & (seam_owner[:, None, :] == myself)
    send_strip = jnp.sum(jnp.where(as_owner, seam_row[:, None, :], 0), axis=2)
    send_active = jnp.any(as_owner, axis=2)
    own_owner = lax.dynamic_index_in_dim(seam_owner, myself, 0, keepdims=False)
    own_to = lax.dynamic_index_in_dim(seam_to, myself, 0, keepdims=False)
    own_ordinal = lax.dynamic_index_in_dim(ordinal, myself, 0, keepdims=False)
    landing = (own_to[:, None] == jnp.arange(strips)[None, :]).astype(jnp.float32)
    return (send_strip, send_active, own_owner, own_to, own_ordinal, landing)


def receiver_side(tables, owner_ids):
    own_owner, own_to, own_ordinal, landing = (tables[2], tables[3], tables[4], tables[5])
    match_slot = (
        (own_owner[:, None, None] >= 0)
        & (own_owner[:, None, None] == owner_ids[None, :, None])
        & (own_ordinal[:, None, None] == jnp.arange(SEAM_CAP)[None, None, :])
    )
    matrix = jnp.einsum("kt,kqr->tqr", landing, match_slot.astype(jnp.float32))
    back_strip = jnp.sum(jnp.where(match_slot, own_to[:, None, None], 0), axis=0)
    return (matrix, back_strip)


def sender_side(tables, receiver_ids, strips):
    send_strip, send_active = (tables[0], tables[1])
    tile_count = send_strip.shape[0]
    inside_range = (receiver_ids >= 0) & (receiver_ids < tile_count)
    clipped = jnp.clip(receiver_ids, 0, tile_count - 1)
    hot = (clipped[:, None] == jnp.arange(tile_count)[None, :])[:, :, None]
    strip_ids = jnp.sum(jnp.where(hot, send_strip[None], 0), axis=1)
    live_ids = jnp.any(hot & send_active[None], axis=1) & inside_range[:, None]
    matrix = ((strip_ids[None] == jnp.arange(strips)[:, None, None]) & live_ids[None]).astype(
        jnp.float32
    )
    return (strip_ids, matrix)


def pick_strips(values, strip_ids):
    hot = (strip_ids.reshape(-1)[:, None] == jnp.arange(values.shape[1])[None, :]).astype(
        values.dtype
    )
    gathered = jnp.einsum(
        "qs,fscp->fqcp", hot, values, preferred_element_type=jnp.float32
    ).astype(values.dtype)
    return gathered.reshape(
        values.shape[0], strip_ids.shape[0], strip_ids.shape[1], values.shape[2], values.shape[3]
    )


def place_strips(received, matrix):
    return jnp.einsum(
        "tqr,fqrcp->ftcp", matrix.astype(jnp.bfloat16), received, preferred_element_type=jnp.float32
    )


def exchange_sum(parts, axes):
    flat = jnp.concatenate([part.reshape(-1) for part in parts])
    size = 1
    for axis in axes:
        size *= lax.axis_size(axis)
    pieces = flat.reshape(size, -1)
    flat = jnp.sum(lax.all_to_all(pieces, axes, 0, 0, tiled=True), axis=0)
    copies = jnp.broadcast_to(flat[None], (size,) + flat.shape)
    flat = lax.all_to_all(copies, axes, 0, 0, tiled=True).reshape(-1)
    results = []
    start = 0
    for part in parts:
        results.append(flat[start : start + part.size].reshape(part.shape))
        start += part.size
    return results


def shards(
    features,
    spatial_a,
    first_time_kernel,
    spatial_b,
    second_time_kernel,
    seam_owner,
    seam_row,
    seam_to,
    grad_out,
):
    total_frames = features.shape[0] * lax.axis_size("frame")
    wide_dilation = min(8, total_frames // 4)
    strips = features.shape[1]
    first_layer, pre_one, padded_zero = spatial_forward(features, spatial_a, chart_rim)
    second_layer, second_preactivation, first_padded = time_kernel_forward(
        first_layer, first_time_kernel, NEAR_DILATION
    )
    frames_three, pre_three, padded_two = spatial_forward(second_layer, spatial_b, chart_rim)
    frames_four, fourth_preactivation, third_padded = time_kernel_forward(
        frames_three, second_time_kernel, wide_dilation
    )
    tables = seam_tables(seam_owner, seam_row, seam_to, strips)
    myself = lax.axis_index("chart")
    offsets = [offset for offset in range(-REACH, REACH + 1) if offset != 0]
    offset_array = jnp.array(offsets, dtype=jnp.int32)
    receive_matrix, back_strip = receiver_side(tables, myself + offset_array)
    outgoing = {}
    for position, offset in enumerate(offsets):
        strip_ids, unused_matrix = sender_side(tables, jnp.reshape(myself - offset, (1,)), strips)
        outgoing[offset] = pick_strips(frames_four, strip_ids)
    arrivals = {}
    returns = {}
    for position, offset in enumerate(offsets):
        going_back = pick_strips(grad_out, back_strip[position : position + 1])
        payload = jnp.concatenate([outgoing[-offset], going_back], axis=1)
        landed = near_send(payload, offset)
        arrivals[-offset] = landed[:, :1]
        returns[offset] = landed[:, 1:]
    moved = place_strips(
        jnp.concatenate([arrivals[offset] for offset in offsets], axis=1), receive_matrix
    )
    unused_ids, return_matrix = sender_side(tables, myself - offset_array, strips)
    moved_back = place_strips(
        jnp.concatenate([returns[offset] for offset in offsets], axis=1), return_matrix
    )
    blended = (frames_four.astype(jnp.float32) + moved).astype(jnp.bfloat16)
    fourth_gradient = (grad_out.astype(jnp.float32) + moved_back).astype(jnp.bfloat16)
    third_gradient, gradient_kernel_second = temporal_backward(
        fourth_gradient,
        fourth_preactivation,
        third_padded,
        second_time_kernel,
        wide_dilation,
    )
    frames_grad_two, grad_sb = spatial_backward(
        third_gradient, pre_three, padded_two, spatial_b, chart_rim
    )
    first_gradient, gradient_kernel_first = temporal_backward(
        frames_grad_two,
        second_preactivation,
        first_padded,
        first_time_kernel,
        NEAR_DILATION,
    )
    grad_features, grad_sa = spatial_backward(
        first_gradient, pre_one, padded_zero, spatial_a, chart_rim
    )
    summed_sa, summed_ta, summed_sb, summed_tb = exchange_sum(
        (grad_sa, gradient_kernel_first, grad_sb, gradient_kernel_second), ("frame", "chart")
    )
    pixel_frames = total_frames * strips * lax.axis_size("chart") * features.shape[3]
    grad_scale = float(pixel_frames) ** (-0.5)
    return (
        blended,
        grad_features,
        summed_sa * grad_scale,
        summed_ta * grad_scale,
        summed_sb * grad_scale,
        summed_tb * grad_scale,
    )


def solution(mesh):
    placed = (
        P("frame", "chart", None, None),
        P(),
        P(),
        P(),
        P(),
        P(),
        P(),
        P(),
        P("frame", "chart", None, None),
    )
    return jax.shard_map(
        shards,
        mesh=mesh,
        in_specs=placed,
        out_specs=(
            P("frame", "chart", None, None),
            P("frame", "chart", None, None),
            P(),
            P(),
            P(),
            P(),
        ),
        check_vma=False,
    )
```
